32 devices in a mesh: prow: 8 (over z, x), pcol: 4 (over y, core).
Axes of the slice: x: 2, y: 2, z: 4, core: 2. Of those that a mesh axis runs over, the one named last changes fastest.
Arguments:
- sigma_top: bfloat16 [8, 8, 128, 128], P('prow', 'pcol'), may hold values from -6 to 6
- factor_one: bfloat16 [8, 8, 128, 128], P('prow', 'pcol'), may hold values from -0.1875 to 0.1875
- inverse_one: bfloat16 [8, 128, 128], P('prow'), may hold values from -0.5 to 0.5
- pattern_one: int32 [8, 8], replicated, may hold values from 0 to 7, as said below
- factor_two: bfloat16 [8, 8, 128, 128], P('prow', 'pcol'), may hold values from -0.25 to 0.25
- parent_block: bfloat16 [8, 128, 128], P('prow'), may hold values from -0.25 to 0.25
- inverse_two: bfloat16 [8, 128, 128], P('prow'), may hold values from -0.5 to 0.5
- parent_two: int32 [8], replicated, may hold values from 0 to 7
- keep_two: int32 [8, 8], replicated, may hold values 0 or 1
Outputs:
- inverse_top_one: bfloat16 [8, 8, 128, 128], P('prow')
- diag_one: float32 [8, 128, 128], P('prow')
- inverse_top_two: bfloat16 [8, 8, 128, 128], P('prow')
- inverse_parent_two: float32 [8, 128, 128], P('prow')
- diag_two: float32 [8, 128, 128], P('prow')
The draws below stay inside these ranges and needn't reach their ends.
Inputs may be any that keep to these rules, and one draw needn't show every extreme that they name: Each row of pattern_one lists 8 distinct block rows of the top region. keep_two[i, k] = 1 where level-two supernode i's pattern holds the k-th tile of its parent's pattern. parent_two names level-one supernodes.
All inputs are finite; a program needn't handle non-finite values.
Results may differ from the reference program's by a relative error of at most 0.023.
Values may be sent and summed in bfloat16 or wider, within the bound.
A program may use at most 64 MiB of HBM per device.

```python
import math
import jax
import jax.numpy as jnp
import numpy as np
from jax import lax

W = 128
S = 8
R = 8
NS1 = 8
NS2 = 8
N_PCOL = 4


def draw_pattern_one(key, part):
    keys = jax.random.split(key, NS1)

    def one_row(row_key):
        return jax.random.permutation(row_key, S)[:R]
    return jax.vmap(one_row)(keys).astype(jnp.int32)


def touch_ends(result, key, low, top_value):
    dims = result.shape
    spot = [jax.random.randint(jax.random.fold_in(key, axis), (), 0, dims[axis]) for axis in range(len(dims))]
    result = result.at[tuple(spot)].set(low)
    longest = dims.index(max(dims))
    spot[longest] = (spot[longest] + 1) % dims[longest]
    return result.at[tuple(spot)].set(top_value)


def level_of(key, extent, shards, smallest, top_value):
    def one(dim, blocks):
        draws = jax.random.uniform(jax.random.fold_in(jax.random.fold_in(key, 6), dim), (blocks,), jnp.float32, smallest / len(shards), top_value / len(shards))
        return jnp.repeat(jnp.exp(draws), extent[dim] // blocks).reshape((-1,) + (1,) * (len(extent) - dim - 1))

    loudness = one(*shards[0])
    for cut in shards[1:]:
        loudness = loudness * one(*cut)
    return loudness


def rank_table(count, slope):
    weights = [(1 << 20) // math.isqrt(standing ** slope) + 1 for standing in range(1, count + 1)]
    scale = 1 + sum(weights) // (1 << 30)
    return np.cumsum(np.array([max(1, weight // scale) for weight in weights]))


def ranked_ids(rng, extent, count, slope):
    grid = rank_table(count, slope)
    pick = jax.random.randint(jax.random.fold_in(rng, 1), extent, 0, int(grid[count - 1]))
    standing = jnp.searchsorted(jnp.asarray(grid, jnp.int32), pick, side="right")
    return jax.random.permutation(jax.random.fold_in(rng, 2), count)[standing].astype(jnp.int32)


def centred(own_key, dims, scale, reach, shards=(), kind=jnp.bfloat16):
    drawn = scale * jax.random.normal(own_key, dims, jnp.float32)
    if shards:
        drawn = drawn * level_of(own_key, dims, shards, -0.22, 0.18)
    return jnp.clip(drawn, -reach, reach).astype(kind)


def setup_inputs(seed: int = 0) -> dict:
    seeds = jax.random.split(jax.random.key(seed), 10)
    sigma_top = centred(seeds[0], (S, S, W, W), 1.0, 6.0, ((0, 8), (1, 4)))
    factor_one = centred(seeds[1], (NS1, R, W, W), (R * W) ** -0.5, 0.1875, ((0, 8), (1, 4)))
    inverse_one = centred(seeds[2], (NS1, W, W), W ** -0.5, 0.5, ((0, 8),))
    pattern_one = draw_pattern_one(jax.random.fold_in(seeds[9], 71), 0)
    factor_two = centred(seeds[4], (NS2, R, W, W), ((R // 2 + 1) * W) ** -0.5, 0.25, ((0, 8), (1, 4)))
    parent_block = centred(seeds[5], (NS2, W, W), ((R // 2 + 1) * W) ** -0.5, 0.25, ((0, 8),))
    inverse_two = centred(seeds[6], (NS2, W, W), W ** -0.5, 0.5, ((0, 8),))
    parent_two = touch_ends(ranked_ids(seeds[7], (NS2,), NS1, 2), jax.random.fold_in(seeds[7], 3), 0, NS1 - 1).astype(jnp.int32)
    keep_two = touch_ends((jax.random.randint(seeds[8], (NS2, R), 0, 2) < 1).astype(jnp.int32), jax.random.fold_in(seeds[8], 1), 0, 1)
    return dict(sigma_top=sigma_top, factor_one=factor_one, inverse_one=inverse_one, pattern_one=pattern_one, factor_two=factor_two, parent_block=parent_block, inverse_two=inverse_two, parent_two=parent_two, keep_two=keep_two)


highest = lax.Precision.HIGHEST


def column_sums(sigma_top, spread, extra):
    group = S // N_PCOL
    count = spread.shape[1]
    total = jnp.zeros((S, count, W, W), jnp.float32)
    top_rows = jnp.arange(S, dtype=jnp.int32) // group
    for column in range(N_PCOL):
        block = sigma_top[:, column * group:(column + 1) * group].astype(jnp.float32)
        piece = spread[column * group:(column + 1) * group].astype(jnp.float32)
        part = jnp.einsum("abwv,bjvx->ajwx", block, piece, precision=highest)
        if extra is not None:
            inside = (top_rows == column).astype(jnp.float32)[:, None, None, None]
            part = part + inside * extra
        rounded = lax.optimization_barrier(part.astype(jnp.bfloat16))
        total = total + rounded.astype(jnp.float32)
    return total


def reference(sigma_top, factor_one, inverse_one, pattern_one, factor_two, parent_block, inverse_two, parent_two, keep_two):
    top_ids = jnp.arange(S, dtype=jnp.int32)
    lower_one = jnp.tril(inverse_one).astype(jnp.float32)
    scaled_one = jnp.einsum("jkwv,jvx->jkwx", factor_one.astype(jnp.float32), lower_one, precision=highest).astype(jnp.bfloat16)
    picker_one = (pattern_one[:, :, None] == top_ids[None, None, :]).astype(jnp.float32)
    spread_one = jnp.einsum("jkb,jkwv->bjwv", picker_one, scaled_one.astype(jnp.float32), precision=highest).astype(jnp.bfloat16)
    summed_one = column_sums(sigma_top, spread_one, None)
    member_one = jnp.sum(picker_one, axis=1).T
    inverse_top_one = (-summed_one * member_one[:, :, None, None]).astype(jnp.bfloat16)
    diag_one = jnp.einsum("jwv,jwx->jvx", lower_one, lower_one, precision=highest)
    diag_one = diag_one + jnp.einsum("ajwv,ajwx->jvx", spread_one.astype(jnp.float32), summed_one, precision=highest)

    lower_two = jnp.tril(inverse_two).astype(jnp.float32)
    scaled_two = jnp.einsum("ikwv,ivx->ikwx", factor_two.astype(jnp.float32), lower_two, precision=highest).astype(jnp.bfloat16)
    scaled_parent = jnp.einsum("iwv,ivx->iwx", parent_block.astype(jnp.float32), lower_two, precision=highest).astype(jnp.bfloat16)
    parent_hot = (parent_two[:, None] == jnp.arange(NS1, dtype=jnp.int32)[None, :]).astype(jnp.int32)
    parent_pattern = jnp.sum(parent_hot[:, :, None] * pattern_one[None, :, :], axis=1)
    picker_two = (parent_pattern[:, :, None] == top_ids[None, None, :]).astype(jnp.float32) * keep_two[:, :, None].astype(jnp.float32)
    spread_two = jnp.einsum("ikb,ikwv->biwv", picker_two, scaled_two.astype(jnp.float32), precision=highest).astype(jnp.bfloat16)
    inherited = jnp.einsum("ij,ajwv->aiwv", parent_hot.astype(jnp.float32), inverse_top_one.astype(jnp.float32), precision=highest).astype(jnp.bfloat16)
    parent_float = scaled_parent.astype(jnp.float32)
    extra = jnp.einsum("aiwv,ivx->aiwx", inherited.astype(jnp.float32), parent_float, precision=highest)
    summed_two = column_sums(sigma_top, spread_two, extra)
    member_two = jnp.sum(picker_two, axis=1).T
    inverse_top_two = (-summed_two * member_two[:, :, None, None]).astype(jnp.bfloat16)
    cross = jnp.einsum("biwv,biwx->ivx", inherited.astype(jnp.float32), spread_two.astype(jnp.float32), precision=highest)
    parent_diag = jnp.einsum("ij,jwv->iwv", parent_hot.astype(jnp.float32), diag_one, precision=highest)
    carried = cross + jnp.einsum("iwv,ivx->iwx", parent_diag, parent_float, precision=highest)
    diag_two = jnp.einsum("iwv,iwx->ivx", lower_two, lower_two, precision=highest)
    diag_two = diag_two + jnp.einsum("aiwv,aiwx->ivx", spread_two.astype(jnp.float32), summed_two, precision=highest)
    diag_two = diag_two + jnp.einsum("iwv,iwx->ivx", parent_float, carried, precision=highest)
    return inverse_top_one, diag_one, inverse_top_two, -carried, diag_two
```

```python
import functools

import jax
import jax.numpy as jnp
from jax import lax
from jax.experimental import pallas as pl
from jax.experimental.pallas import tpu as pltpu
from jax.sharding import PartitionSpec as P

MESH = pl.DeviceIdType.MESH
f32 = jnp.float32
bf16 = jnp.bfloat16


def each(count, step, start=0):
    if count - start <= 8:
        for i in range(start, count):
            step(i)
    else:
        lax.fori_loop(start, count, lambda i, carry: (step(i), carry)[1], 0)


def dot(left, right):
    return jnp.dot(left, right, preferred_element_type=f32)


def dot_t(left, right):
    return dot(left.astype(f32).T.astype(bf16), right)


def kernel(
    prows, pcols, group,
    sigma, factor_one, inverse_one, factor_two, parent_block, inverse_two,
    pattern, parent, keep,
    top_one, diag_one, top_two, parent_out, diag_two,
    msg, par_msg, rx, par_rx, sig, spread, total, ag, two_send, two_recv, z_one, z_two, zr_one, zr_two, fin,
    msg_s, par_s, msg_r, par_r, sig_s, sig_r, ag_s, ag_r, two_s, two_r, z_s, zr_one_r, zr_two_r, fin_s, fin_r,
):
    planes = prows // group
    half = pcols // 2
    cols = sigma.shape[1]
    w = sigma.shape[2]
    tiles = factor_one.shape[1]
    reach = pattern.shape[1]
    tops = prows
    members = group * pcols
    slice_rows = w // pcols

    p = lax.axis_index("prow")
    c = lax.axis_index("pcol")
    z, x = p // group, p % group
    m = x * pcols + c
    home = c // 2 + (c % 2) * half
    j = home * group + x
    mine = p == j
    target_col = (z % half) * 2 + z // half

    def place(row):
        plane = row // group
        return (row % group) * pcols + (plane % half) * 2 + plane // half

    def peer(t):
        q = (m + t) % members
        return q, (z * group + q // pcols, q % pcols)

    barrier = pltpu.get_barrier_semaphore()

    def greet_plane(t):
        pl.semaphore_signal(barrier, inc=1, device_id=peer(t)[1], device_id_type=MESH)

    def greet_line(t):
        other = (z + 1 + t // pcols) % planes
        pl.semaphore_signal(
            barrier, inc=1, device_id=(other * group + x, t % pcols), device_id_type=MESH
        )

    each((planes - 1) * pcols, greet_line)
    each(members, greet_plane, 1)

    keep_lower = lax.broadcasted_iota(jnp.int32, (w, w), 0) >= lax.broadcasted_iota(
        jnp.int32, (w, w), 1
    )
    lower_one = jnp.where(keep_lower, inverse_one[0].astype(f32), 0.0).astype(bf16)
    lower_two = jnp.where(keep_lower, inverse_two[0].astype(f32), 0.0).astype(bf16)
    for k in range(tiles):
        msg[k] = dot(factor_one[0, k], lower_one).astype(bf16)
        msg[tiles + k] = dot(factor_two[0, k], lower_two).astype(bf16)
    part = parent_block[0, pl.ds(pl.multiple_of(c * slice_rows, slice_rows), slice_rows), :]
    par_msg[...] = dot(part, lower_two).astype(bf16)
    own_cols = pl.ds(c * cols, cols)
    sig[x, own_cols] = sigma[0]

    pl.semaphore_wait(barrier, (planes - 1) * pcols + members - 1)

    def msg_copy(t):
        other = (z + t) % planes
        return pltpu.make_async_remote_copy(
            src_ref=msg, dst_ref=rx.at[c], send_sem=msg_s.at[t], recv_sem=msg_r.at[c],
            device_id=(other * group + x, target_col), device_id_type=MESH,
        )

    def par_copy(t):
        other = (z + t) % planes
        return pltpu.make_async_remote_copy(
            src_ref=par_msg, dst_ref=par_rx.at[c], send_sem=par_s.at[t], recv_sem=par_r.at[c],
            device_id=(other * group + x, target_col), device_id_type=MESH,
        )

    stays = target_col == c
    for copy_to in (msg_copy, par_copy):
        each(planes, lambda t: copy_to(planes - t).start(), 1)

    @pl.when(jnp.logical_not(stays))
    def _():
        msg_copy(0).start()
        par_copy(0).start()

    @pl.when(stays)
    def _():
        pltpu.make_async_copy(msg, rx.at[c], msg_r.at[c]).start()
        pltpu.make_async_copy(par_msg, par_rx.at[c], par_r.at[c]).start()

    def sig_copy(t):
        return pltpu.make_async_remote_copy(
            src_ref=sigma.at[0], dst_ref=sig.at[x, own_cols], send_sem=sig_s.at[t],
            recv_sem=sig_r.at[m], device_id=peer(t)[1], device_id_type=MESH,
        )

    each(members, lambda t: sig_copy(t).start(), 1)

    def gram(lower):
        return jnp.where(mine, dot_t(lower, lower), 0.0)

    gram_one = gram(lower_one)
    gram_two = gram(lower_two)

    each(pcols, lambda t: pltpu.make_async_copy(rx.at[t], rx.at[t], msg_r.at[t]).wait())
    each(pcols, lambda t: pltpu.make_async_copy(par_rx.at[t], par_rx.at[t], par_r.at[t]).wait())

    up = parent[j]
    rows_one = [pattern[j, k] for k in range(reach)]
    rows_two = [pattern[up, k] for k in range(reach)]
    kept = [keep[j, k] for k in range(reach)]

    def find(rows, weights, b):
        column = tile = hit = jnp.int32(0)
        for k in range(reach):
            same = rows[k] == b
            if weights is not None:
                same = jnp.logical_and(same, weights[k] == 1)
            column = jnp.where(same, k // tiles, column)
            tile = jnp.where(same, k % tiles, tile)
            hit = jnp.where(same, 1, hit)
        return column, tile, hit.astype(f32)

    def fill(b):
        rows = pl.ds(pl.multiple_of(b * w, w), w)
        column, tile, hit = find(rows_one, None, b)
        spread[rows, 0:w] = (rx[column, tile].astype(f32) * hit).astype(bf16)
        column, tile, hit = find(rows_two, kept, b)
        spread[rows, w:2 * w] = (rx[column, tiles + tile].astype(f32) * hit).astype(bf16)

    each(tops, fill)
    scaled_parent = jnp.concatenate(
        [par_rx[t] for t in range(pcols)], axis=0
    )

    def sig_wait(t):
        q, _ = peer(t)
        ref = sig.at[q // pcols, pl.ds((q % pcols) * cols, cols)]
        pltpu.make_async_copy(ref, ref, sig_r.at[q]).wait()

    each(members, sig_wait, 1)

    chunk = 8 if tops % 8 == 0 else 1

    def product(b0):
        return [
            dot(
                jnp.concatenate([sig[g, b0 + b] for b in range(chunk)], axis=1),
                spread[pl.ds(pl.multiple_of(b0 * w, w), chunk * w), :],
            )
            for g in range(group)
        ]

    if tops == chunk:
        sums = product(0)
    else:
        total[...] = jnp.zeros_like(total)

        def add(n):
            for g, value in enumerate(product(n * chunk)):
                total[g] += value

        lax.fori_loop(0, tops // chunk, lambda n, carry: (add(n), carry)[1], 0)
        sums = [total[g] for g in range(group)]

    hits_one = [find(rows_one, None, z * group + g)[2] for g in range(group)]
    hits_two = [find(rows_two, kept, z * group + g)[2] for g in range(group)]
    own_rows = spread[pl.ds(pl.multiple_of(z * group * w, w), group * w), :]
    own_one, own_two = own_rows[:, 0:w], own_rows[:, w:2 * w]
    summed_one = jnp.concatenate([s[:, 0:w] for s in sums], axis=0)
    for g in range(group):
        ag[m, g] = (sums[g][:, 0:w] * -hits_one[g]).astype(bf16)
    part_one = (gram_one + dot_t(own_one, summed_one.astype(bf16))).astype(bf16)
    ag[m, group] = part_one
    z_one[...] = part_one

    def ag_copy(t):
        return pltpu.make_async_remote_copy(
            src_ref=ag.at[m], dst_ref=ag.at[m], send_sem=ag_s.at[t], recv_sem=ag_r.at[m],
            device_id=peer(t)[1], device_id_type=MESH,
        )

    each(members, lambda t: ag_copy(t).start(), 1)

    def z_copy(source, target, sem, recv):
        return pltpu.make_async_remote_copy(
            src_ref=source, dst_ref=target.at[z], send_sem=z_s.at[sem], recv_sem=recv.at[z],
            device_id=(home * group + x, c), device_id_type=MESH,
        )

    first = z_copy(z_one, zr_one, 0, zr_one_r)
    second = z_copy(z_two, zr_two, 1, zr_two_r)

    @pl.when(jnp.logical_not(mine))
    def _():
        first.start()

    def ag_wait(t):
        q, _ = peer(t)
        pltpu.make_async_copy(ag.at[q], ag.at[q], ag_r.at[q]).wait()

    each(members, ag_wait, 1)

    slot = jnp.int32(0)
    for row in range(tops):
        slot = jnp.where(up == row, place(row), slot)
    inherited = jnp.concatenate([ag[slot, g] for g in range(group)], axis=0)
    up_diag = ag[slot, group]
    summed_two = jnp.concatenate([s[:, w:2 * w] for s in sums], axis=0) + dot(
        inherited, scaled_parent
    )
    carried = dot_t(inherited, own_two) + dot(up_diag, scaled_parent)
    part_two = (
        gram_two
        + dot_t(own_two, summed_two.astype(bf16))
        + dot_t(scaled_parent, carried.astype(bf16))
    )
    z_two[0] = carried.astype(bf16)
    z_two[1] = part_two.astype(bf16)

    @pl.when(jnp.logical_not(mine))
    def _():
        second.start()

    for g in range(group):
        two_send[g] = (summed_two[g * w:(g + 1) * w] * -hits_two[g]).astype(bf16)
    two_recv[m] = two_send[x]

    def two_copy(t):
        q, device = peer(t)
        return pltpu.make_async_remote_copy(
            src_ref=two_send.at[q // pcols], dst_ref=two_recv.at[m], send_sem=two_s.at[t],
            recv_sem=two_r.at[m], device_id=device, device_id_type=MESH,
        )

    each(members, lambda t: two_copy(t).start(), 1)

    def fin_copy(t):
        return pltpu.make_async_remote_copy(
            src_ref=fin, dst_ref=fin, send_sem=fin_s.at[t], recv_sem=fin_r,
            device_id=(p, (c + t) % pcols), device_id_type=MESH,
        )

    @pl.when(mine)
    def _():
        def gather_wait(ref, sem):
            def step(t):
                other = (z + t) % planes
                pltpu.make_async_copy(ref.at[other], ref.at[other], sem.at[other]).wait()
            each(planes, step, 1)

        gather_wait(zr_one, zr_one_r)
        zr_one[z] = z_one[...]
        fin[0] = jnp.sum(zr_one[...].astype(f32), axis=0).astype(bf16)
        gather_wait(zr_two, zr_two_r)
        zr_two[z] = z_two[...]
        fin[1:3] = jnp.sum(zr_two[...].astype(f32), axis=0).astype(bf16)
        each(pcols, lambda t: fin_copy(t).start(), 1)

    def out_one(row):
        top_one[0, row] = ag[place(row), x]

    each(tops, out_one)

    def two_wait(t):
        q, _ = peer(t)
        pltpu.make_async_copy(two_recv.at[q], two_recv.at[q], two_r.at[q]).wait()

    each(members, two_wait, 1)

    def out_two(row):
        top_two[0, row] = two_recv[place(row)]

    each(tops, out_two)

    @pl.when(jnp.logical_not(mine))
    def _():
        pltpu.make_async_copy(fin, fin, fin_r).wait()

    diag_one[0] = fin[0].astype(f32)
    parent_out[0] = -fin[1].astype(f32)
    diag_two[0] = fin[2].astype(f32)

    for copy_to in (msg_copy, par_copy):
        each(planes, lambda t: copy_to(planes - t).wait_send(), 1)

    @pl.when(jnp.logical_not(stays))
    def _():
        msg_copy(0).wait_send()
        par_copy(0).wait_send()

    def drain(t):
        sig_copy(t).wait_send()
        ag_copy(t).wait_send()
        two_copy(t).wait_send()

    each(members, drain, 1)

    @pl.when(jnp.logical_not(mine))
    def _():
        first.wait_send()
        second.wait_send()

    @pl.when(mine)
    def _():
        each(pcols, lambda t: fin_copy(t).wait_send(), 1)


def body(
    prows, pcols,
    sigma_top, factor_one, inverse_one, pattern_one, factor_two, parent_block, inverse_two,
    parent_two, keep_two,
):
    w = sigma_top.shape[2]
    total_one = pattern_one.shape[0]
    tops = prows * sigma_top.shape[0]
    group = total_one // pcols
    planes = prows // group
    members = group * pcols
    tiles = factor_one.shape[1]
    assert sigma_top.shape[0] == factor_one.shape[0] == factor_two.shape[0] == 1
    assert planes == pcols and members == tops == total_one == parent_two.shape[0]
    vmem = pl.BlockSpec(memory_space=pltpu.VMEM)
    smem = pl.BlockSpec(memory_space=pltpu.SMEM)
    dma = pltpu.SemaphoreType.DMA
    return pl.pallas_call(
        functools.partial(kernel, prows, pcols, group),
        out_shape=(
            jax.ShapeDtypeStruct((1, total_one, w, w), bf16),
            jax.ShapeDtypeStruct((1, w, w), f32),
            jax.ShapeDtypeStruct((1, total_one, w, w), bf16),
            jax.ShapeDtypeStruct((1, w, w), f32),
            jax.ShapeDtypeStruct((1, w, w), f32),
        ),
        in_specs=[vmem] * 6 + [smem] * 3,
        out_specs=(vmem,) * 5,
        scratch_shapes=[
            pltpu.VMEM((2 * tiles, w, w), bf16),
            pltpu.VMEM((w // pcols, w), bf16),
            pltpu.VMEM((pcols, 2 * tiles, w, w), bf16),
            pltpu.VMEM((pcols, w // pcols, w), bf16),
            pltpu.VMEM((group, tops, w, w), bf16),
            pltpu.VMEM((tops * w, 2 * w), bf16),
            pltpu.VMEM((group, w, 2 * w), f32),
            pltpu.VMEM((members, group + 1, w, w), bf16),
            pltpu.VMEM((group, w, w), bf16),
            pltpu.VMEM((members, w, w), bf16),
            pltpu.VMEM((w, w), bf16),
            pltpu.VMEM((2, w, w), bf16),
            pltpu.VMEM((planes, w, w), bf16),
            pltpu.VMEM((planes, 2, w, w), bf16),
            pltpu.VMEM((3, w, w), bf16),
            dma((planes,)), dma((planes,)), dma((pcols,)), dma((pcols,)),
            dma((members,)), dma((members,)),
            dma((members,)), dma((members,)),
            dma((members,)), dma((members,)),
            dma((2,)), dma((planes,)), dma((planes,)),
            dma((pcols,)), dma,
        ],
        compiler_params=pltpu.CompilerParams(
            collective_id=0, has_side_effects=True, vmem_limit_bytes=40 * 1024 * 1024
        ),
    )(
        sigma_top, factor_one, inverse_one, factor_two, parent_block, inverse_two,
        pattern_one, parent_two, keep_two,
    )


def solution(mesh):
    in_specs = (
        P("prow", "pcol", None, None),
        P("prow", "pcol", None, None),
        P("prow", None, None),
        P(),
        P("prow", "pcol", None, None),
        P("prow", None, None),
        P("prow", None, None),
        P(),
        P(),
    )
    out_specs = (
        P("prow", None, None, None),
        P("prow", None, None),
        P("prow", None, None, None),
        P("prow", None, None),
        P("prow", None, None),
    )
    step = functools.partial(body, mesh.shape["prow"], mesh.shape["pcol"])
    return jax.shard_map(step, mesh=mesh, in_specs=in_specs, out_specs=out_specs, check_vma=False)
```

```python
import functools

import jax
import jax.numpy as jnp
from jax import lax
from jax.experimental import pallas as pl
from jax.experimental.pallas import tpu as pltpu
from jax.sharding import PartitionSpec as P

MESH = pl.DeviceIdType.MESH
f32 = jnp.float32
bf16 = jnp.bfloat16


def each(count, step, start=0):
    if count - start <= 8:
        for i in range(start, count):
            step(i)
    else:
        lax.fori_loop(start, count, lambda i, carry: (step(i), carry)[1], 0)


def dot(left, right):
    return jnp.dot(left, right, preferred_element_type=f32)


def dot_t(left, right):
    return dot(left.astype(f32).T.astype(bf16), right)


def kernel(
    prows, pcols, group,
    sigma, factor_one_in, inverse_one_in, factor_two_in, parent_block_in, inverse_two_in,
    pattern_in, parent_in, keep_in,
    top_one, diag_one, top_two, parent_out, diag_two,
    factor_one, inverse_one, factor_two, parent_block, inverse_two, pattern, parent, keep,
    load_s, store_s, blocks, msg, par_msg, rx, par_rx, sig, spread, total, ag, two_send, two_recv, z_one, z_two, zr_one, zr_two, fin,
    msg_s, par_s, msg_r, par_r, sig_s, sig_r, ag_s, ag_r, two_s, two_r, z_s, zr_one_r, zr_two_r, fin_s, fin_r,
):
    planes = prows // group
    half = pcols // 2
    cols = sigma.shape[1]
    w = sigma.shape[2]
    tiles = factor_one_in.shape[1]
    reach = pattern.shape[1]
    tops = prows
    members = group * pcols
    slice_rows = w // pcols

    p = lax.axis_index("prow")
    c = lax.axis_index("pcol")
    z, x = p // group, p % group
    m = x * pcols + c
    home = c // 2 + (c % 2) * half
    j = home * group + x
    mine = p == j
    target_col = (z % half) * 2 + z // half

    def place(row):
        plane = row // group
        return (row % group) * pcols + (plane % half) * 2 + plane // half

    def peer(t):
        q = (m + t) % members
        return q, (z * group + q // pcols, q % pcols)

    own_cols = pl.ds(c * cols, cols)
    loads = [
        pltpu.make_async_copy(source, target, load_s.at[n])
        for n, (source, target) in enumerate([
            (inverse_two_in, inverse_two), (factor_two_in, factor_two),
            (inverse_one_in, inverse_one), (factor_one_in, factor_one),
            (parent_block_in, parent_block), (sigma.at[0], sig.at[x, own_cols]),
            (pattern_in, pattern), (parent_in, parent), (keep_in, keep),
        ])
    ]
    for load in loads:
        load.start()

    barrier = pltpu.get_barrier_semaphore()

    def greet_plane(t):
        pl.semaphore_signal(barrier, inc=1, device_id=peer(t)[1], device_id_type=MESH)

    def greet_line(t):
        other = (z + 1 + t // pcols) % planes
        pl.semaphore_signal(
            barrier, inc=1, device_id=(other * group + x, t % pcols), device_id_type=MESH
        )

    each((planes - 1) * pcols, greet_line)
    each(members, greet_plane, 1)

    for load in loads:
        load.wait()

    keep_lower = lax.broadcasted_iota(jnp.int32, (w, w), 0) >= lax.broadcasted_iota(
        jnp.int32, (w, w), 1
    )
    lower_one = jnp.where(keep_lower, inverse_one[0].astype(f32), 0.0).astype(bf16)
    lower_two = jnp.where(keep_lower, inverse_two[0].astype(f32), 0.0).astype(bf16)
    for k in range(tiles):
        msg[k] = dot(factor_one[0, k], lower_one).astype(bf16)
        msg[tiles + k] = dot(factor_two[0, k], lower_two).astype(bf16)
    part = parent_block[0, pl.ds(pl.multiple_of(c * slice_rows, slice_rows), slice_rows), :]
    par_msg[...] = dot(part, lower_two).astype(bf16)

    pl.semaphore_wait(barrier, (planes - 1) * pcols + members - 1)

    def msg_copy(t):
        other = (z + t) % planes
        return pltpu.make_async_remote_copy(
            src_ref=msg, dst_ref=rx.at[c], send_sem=msg_s.at[t], recv_sem=msg_r.at[c],
            device_id=(other * group + x, target_col), device_id_type=MESH,
        )

    def par_copy(t):
        other = (z + t) % planes
        return pltpu.make_async_remote_copy(
            src_ref=par_msg, dst_ref=par_rx.at[c], send_sem=par_s.at[t], recv_sem=par_r.at[c],
            device_id=(other * group + x, target_col), device_id_type=MESH,
        )

    stays = target_col == c
    for copy_to in (msg_copy, par_copy):
        each(planes, lambda t: copy_to(planes - t).start(), 1)

    @pl.when(jnp.logical_not(stays))
    def _():
        msg_copy(0).start()
        par_copy(0).start()

    @pl.when(stays)
    def _():
        pltpu.make_async_copy(msg, rx.at[c], msg_r.at[c]).start()
        pltpu.make_async_copy(par_msg, par_rx.at[c], par_r.at[c]).start()

    def sig_copy(t):
        return pltpu.make_async_remote_copy(
            src_ref=sigma.at[0], dst_ref=sig.at[x, own_cols], send_sem=sig_s.at[t],
            recv_sem=sig_r.at[m], device_id=peer(t)[1], device_id_type=MESH,
        )

    each(members, lambda t: sig_copy(t).start(), 1)

    def gram(lower):
        return jnp.where(mine, dot_t(lower, lower), 0.0)

    gram_one = gram(lower_one)
    gram_two = gram(lower_two)

    each(pcols, lambda t: pltpu.make_async_copy(rx.at[t], rx.at[t], msg_r.at[t]).wait())
    each(pcols, lambda t: pltpu.make_async_copy(par_rx.at[t], par_rx.at[t], par_r.at[t]).wait())

    up = parent[j]
    rows_one = [pattern[j, k] for k in range(reach)]
    rows_two = [pattern[up, k] for k in range(reach)]
    kept = [keep[j, k] for k in range(reach)]

    def find(rows, weights, b):
        column = tile = hit = jnp.int32(0)
        for k in range(reach):
            same = rows[k] == b
            if weights is not None:
                same = jnp.logical_and(same, weights[k] == 1)
            column = jnp.where(same, k // tiles, column)
            tile = jnp.where(same, k % tiles, tile)
            hit = jnp.where(same, 1, hit)
        return column, tile, hit.astype(f32)

    def fill(b):
        rows = pl.ds(pl.multiple_of(b * w, w), w)
        column, tile, hit = find(rows_one, None, b)
        spread[rows, 0:w] = (rx[column, tile].astype(f32) * hit).astype(bf16)
        column, tile, hit = find(rows_two, kept, b)
        spread[rows, w:2 * w] = (rx[column, tiles + tile].astype(f32) * hit).astype(bf16)

    each(tops, fill)
    scaled_parent = jnp.concatenate(
        [par_rx[t] for t in range(pcols)], axis=0
    )

    def sig_wait(t):
        q, _ = peer(t)
        ref = sig.at[q // pcols, pl.ds((q % pcols) * cols, cols)]
        pltpu.make_async_copy(ref, ref, sig_r.at[q]).wait()

    each(members, sig_wait, 1)

    chunk = 8 if tops % 8 == 0 else 1

    def product(b0):
        return [
            dot(
                jnp.concatenate([sig[g, b0 + b] for b in range(chunk)], axis=1),
                spread[pl.ds(pl.multiple_of(b0 * w, w), chunk * w), :],
            )
            for g in range(group)
        ]

    if tops == chunk:
        sums = product(0)
    else:
        total[...] = jnp.zeros_like(total)

        def add(n):
            for g, value in enumerate(product(n * chunk)):
                total[g] += value

        lax.fori_loop(0, tops // chunk, lambda n, carry: (add(n), carry)[1], 0)
        sums = [total[g] for g in range(group)]

    hits_one = [find(rows_one, None, z * group + g)[2] for g in range(group)]
    hits_two = [find(rows_two, kept, z * group + g)[2] for g in range(group)]
    own_rows = spread[pl.ds(pl.multiple_of(z * group * w, w), group * w), :]
    own_one, own_two = own_rows[:, 0:w], own_rows[:, w:2 * w]
    summed_one = jnp.concatenate([s[:, 0:w] for s in sums], axis=0)
    for g in range(group):
        ag[m, g] = (sums[g][:, 0:w] * -hits_one[g]).astype(bf16)
    part_one = (gram_one + dot_t(own_one, summed_one.astype(bf16))).astype(bf16)
    ag[m, group] = part_one
    z_one[...] = part_one

    def ag_copy(t):
        return pltpu.make_async_remote_copy(
            src_ref=ag.at[m], dst_ref=ag.at[m], send_sem=ag_s.at[t], recv_sem=ag_r.at[m],
            device_id=peer(t)[1], device_id_type=MESH,
        )

    each(members, lambda t: ag_copy(t).start(), 1)

    def z_copy(source, target, sem, recv):
        return pltpu.make_async_remote_copy(
            src_ref=source, dst_ref=target.at[z], send_sem=z_s.at[sem], recv_sem=recv.at[z],
            device_id=(home * group + x, c), device_id_type=MESH,
        )

    first = z_copy(z_one, zr_one, 0, zr_one_r)
    second = z_copy(z_two, zr_two, 1, zr_two_r)

    @pl.when(jnp.logical_not(mine))
    def _():
        first.start()

    def ag_wait(t):
        q, _ = peer(t)
        pltpu.make_async_copy(ag.at[q], ag.at[q], ag_r.at[q]).wait()

    each(members, ag_wait, 1)

    def out_one(row):
        return pltpu.make_async_copy(ag.at[place(row), x], top_one.at[0, row], store_s.at[row])

    each(tops, lambda row: out_one(row).start())

    slot = jnp.int32(0)
    for row in range(tops):
        slot = jnp.where(up == row, place(row), slot)
    inherited = jnp.concatenate([ag[slot, g] for g in range(group)], axis=0)
    up_diag = ag[slot, group]
    summed_two = jnp.concatenate([s[:, w:2 * w] for s in sums], axis=0) + dot(
        inherited, scaled_parent
    )
    carried = dot_t(inherited, own_two) + dot(up_diag, scaled_parent)
    part_two = (
        gram_two
        + dot_t(own_two, summed_two.astype(bf16))
        + dot_t(scaled_parent, carried.astype(bf16))
    )
    z_two[0] = carried.astype(bf16)
    z_two[1] = part_two.astype(bf16)

    @pl.when(jnp.logical_not(mine))
    def _():
        second.start()

    for g in range(group):
        two_send[g] = (summed_two[g * w:(g + 1) * w] * -hits_two[g]).astype(bf16)
    two_recv[m] = two_send[x]

    def two_copy(t):
        q, device = peer(t)
        return pltpu.make_async_remote_copy(
            src_ref=two_send.at[q // pcols], dst_ref=two_recv.at[m], send_sem=two_s.at[t],
            recv_sem=two_r.at[m], device_id=device, device_id_type=MESH,
        )

    each(members, lambda t: two_copy(t).start(), 1)

    def fin_copy(t):
        return pltpu.make_async_remote_copy(
            src_ref=fin, dst_ref=fin, send_sem=fin_s.at[t], recv_sem=fin_r,
            device_id=(p, (c + t) % pcols), device_id_type=MESH,
        )

    @pl.when(mine)
    def _():
        def gather_wait(ref, sem):
            def step(t):
                other = (z + t) % planes
                pltpu.make_async_copy(ref.at[other], ref.at[other], sem.at[other]).wait()
            each(planes, step, 1)

        gather_wait(zr_one, zr_one_r)
        zr_one[z] = z_one[...]
        fin[0] = jnp.sum(zr_one[...].astype(f32), axis=0).astype(bf16)
        gather_wait(zr_two, zr_two_r)
        zr_two[z] = z_two[...]
        fin[1:3] = jnp.sum(zr_two[...].astype(f32), axis=0).astype(bf16)
        each(pcols, lambda t: fin_copy(t).start(), 1)


    def two_wait(t):
        q, _ = peer(t)
        pltpu.make_async_copy(two_recv.at[q], two_recv.at[q], two_r.at[q]).wait()

    each(members, two_wait, 1)

    def out_two(row):
        return pltpu.make_async_copy(
            two_recv.at[place(row)], top_two.at[0, row], store_s.at[tops + row]
        )

    each(tops, lambda row: out_two(row).start())

    @pl.when(jnp.logical_not(mine))
    def _():
        pltpu.make_async_copy(fin, fin, fin_r).wait()

    blocks[0] = fin[0].astype(f32)
    blocks[1] = -fin[1].astype(f32)
    blocks[2] = fin[2].astype(f32)
    block_copies = [
        pltpu.make_async_copy(blocks.at[n], ref.at[0], store_s.at[2 * tops + n])
        for n, ref in enumerate((diag_one, parent_out, diag_two))
    ]
    for copy in block_copies:
        copy.start()

    each(tops, lambda row: out_one(row).wait())
    each(tops, lambda row: out_two(row).wait())
    for copy in block_copies:
        copy.wait()
    for copy_to in (msg_copy, par_copy):
        each(planes, lambda t: copy_to(planes - t).wait_send(), 1)

    @pl.when(jnp.logical_not(stays))
    def _():
        msg_copy(0).wait_send()
        par_copy(0).wait_send()

    def drain(t):
        sig_copy(t).wait_send()
        ag_copy(t).wait_send()
        two_copy(t).wait_send()

    each(members, drain, 1)

    @pl.when(jnp.logical_not(mine))
    def _():
        first.wait_send()
        second.wait_send()

    @pl.when(mine)
    def _():
        each(pcols, lambda t: fin_copy(t).wait_send(), 1)


def write_out(*refs):
    copies = [pltpu.make_async_copy(refs[n], refs[5 + n], refs[10].at[n]) for n in range(5)]
    for copy in copies:
        copy.start()
    for copy in copies:
        copy.wait()


def body(
    prows, pcols,
    sigma_top, factor_one, inverse_one, pattern_one, factor_two, parent_block, inverse_two,
    parent_two, keep_two,
):
    w = sigma_top.shape[2]
    total_one = pattern_one.shape[0]
    tops = prows * sigma_top.shape[0]
    group = total_one // pcols
    planes = prows // group
    members = group * pcols
    tiles = factor_one.shape[1]
    assert sigma_top.shape[0] == factor_one.shape[0] == factor_two.shape[0] == 1
    assert planes == pcols and members == tops == total_one == parent_two.shape[0]
    hbm = pl.BlockSpec(memory_space=pltpu.HBM)
    shapes = (
        jax.ShapeDtypeStruct((1, total_one, w, w), bf16),
        jax.ShapeDtypeStruct((1, w, w), f32),
        jax.ShapeDtypeStruct((1, total_one, w, w), bf16),
        jax.ShapeDtypeStruct((1, w, w), f32),
        jax.ShapeDtypeStruct((1, w, w), f32),
    )
    dma = pltpu.SemaphoreType.DMA
    results = pl.pallas_call(
        functools.partial(kernel, prows, pcols, group),
        out_shape=shapes,
        in_specs=[hbm] * 9,
        out_specs=(hbm,) * 5,
        scratch_shapes=[
            pltpu.VMEM(factor_one.shape, bf16),
            pltpu.VMEM(inverse_one.shape, bf16),
            pltpu.VMEM(factor_two.shape, bf16),
            pltpu.VMEM(parent_block.shape, bf16),
            pltpu.VMEM(inverse_two.shape, bf16),
            pltpu.SMEM(pattern_one.shape, jnp.int32),
            pltpu.SMEM(parent_two.shape, jnp.int32),
            pltpu.SMEM(keep_two.shape, jnp.int32),
            dma((9,)),
            dma((2 * total_one + 3,)),
            pltpu.VMEM((3, w, w), f32),
            pltpu.VMEM((2 * tiles, w, w), bf16),
            pltpu.VMEM((w // pcols, w), bf16),
            pltpu.VMEM((pcols, 2 * tiles, w, w), bf16),
            pltpu.VMEM((pcols, w // pcols, w), bf16),
            pltpu.VMEM((group, tops, w, w), bf16),
            pltpu.VMEM((tops * w, 2 * w), bf16),
            pltpu.VMEM((group, w, 2 * w), f32),
            pltpu.VMEM((members, group + 1, w, w), bf16),
            pltpu.VMEM((group, w, w), bf16),
            pltpu.VMEM((members, w, w), bf16),
            pltpu.VMEM((w, w), bf16),
            pltpu.VMEM((2, w, w), bf16),
            pltpu.VMEM((planes, w, w), bf16),
            pltpu.VMEM((planes, 2, w, w), bf16),
            pltpu.VMEM((3, w, w), bf16),
            dma((planes,)), dma((planes,)), dma((pcols,)), dma((pcols,)),
            dma((members,)), dma((members,)),
            dma((members,)), dma((members,)),
            dma((members,)), dma((members,)),
            dma((2,)), dma((planes,)), dma((planes,)),
            dma((pcols,)), dma,
        ],
        compiler_params=pltpu.CompilerParams(
            collective_id=0, has_side_effects=True
        ),
    )(
        sigma_top, factor_one, inverse_one, factor_two, parent_block, inverse_two,
        pattern_one, parent_two, keep_two,
    )
    return pl.pallas_call(
        write_out,
        out_shape=shapes,
        in_specs=[hbm] * 5,
        out_specs=(hbm,) * 5,
        scratch_shapes=[dma((5,))],
    )(*results)


def solution(mesh):
    in_specs = (
        P("prow", "pcol", None, None),
        P("prow", "pcol", None, None),
        P("prow", None, None),
        P(),
        P("prow", "pcol", None, None),
        P("prow", None, None),
        P("prow", None, None),
        P(),
        P(),
    )
    out_specs = (
        P("prow", None, None, None),
        P("prow", None, None),
        P("prow", None, None, None),
        P("prow", None, None),
        P("prow", None, None),
    )
    step = functools.partial(body, mesh.shape["prow"], mesh.shape["pcol"])
    return jax.shard_map(step, mesh=mesh, in_specs=in_specs, out_specs=out_specs, check_vma=False)
```

```python
import functools

import jax
import jax.numpy as jnp
from jax import lax
from jax.experimental import pallas as pl
from jax.experimental.pallas import tpu as pltpu
from jax.sharding import PartitionSpec as P

MESH = pl.DeviceIdType.MESH
f32 = jnp.float32
bf16 = jnp.bfloat16


def each(count, step, start=0):
    if count - start <= 8:
        for i in range(start, count):
            step(i)
    else:
        lax.fori_loop(start, count, lambda i, carry: (step(i), carry)[1], 0)


def dot(left, right):
    return jnp.dot(left, right, preferred_element_type=f32)


def dot_t(left, right):
    return dot(left.astype(f32).T.astype(bf16), right)


def kernel(
    prows, pcols, group,
    sigma, factor_one_in, inverse_one_in, factor_two_in, parent_block_in, inverse_two_in,
    pattern_in, parent_in, keep_in,
    top_one, diag_one, top_two, parent_out, diag_two,
    factor_one, inverse_one, factor_two, parent_block, inverse_two, pattern, parent, keep,
    load_s, store_s, blocks, msg, par_msg, rx, par_rx, sig, spread, total, ag, two_send, two_recv, z_one, z_two, zr_one, zr_two, fin,
    msg_s, par_s, msg_r, par_r, sig_s, sig_r, ag_s, ag_r, two_s, two_r, z_s, zr_one_r, zr_two_r, fin_s, fin_r,
):
    planes = prows // group
    half = pcols // 2
    cols = sigma.shape[1]
    w = sigma.shape[2]
    tiles = factor_one_in.shape[1]
    reach = pattern.shape[1]
    tops = prows
    members = group * pcols
    slice_rows = w // pcols

    p = lax.axis_index("prow")
    c = lax.axis_index("pcol")
    z, x = p // group, p % group
    m = x * pcols + c
    home = c // 2 + (c % 2) * half
    j = home * group + x
    mine = p == j
    target_col = (z % half) * 2 + z // half

    def place(row):
        plane = row // group
        return (row % group) * pcols + (plane % half) * 2 + plane // half

    def peer(t):
        q = (m + t) % members
        return q, (z * group + q // pcols, q % pcols)

    own_cols = pl.ds(c * cols, cols)
    loads = [
        pltpu.make_async_copy(source, target, load_s.at[n])
        for n, (source, target) in enumerate([
            (inverse_two_in, inverse_two), (factor_two_in, factor_two),
            (inverse_one_in, inverse_one), (factor_one_in, factor_one),
            (parent_block_in, parent_block), (sigma.at[0], sig.at[x, own_cols]),
            (pattern_in, pattern), (parent_in, parent), (keep_in, keep),
        ])
    ]
    for load in loads:
        load.start()

    barrier = pltpu.get_barrier_semaphore()

    def greet_plane(t):
        pl.semaphore_signal(barrier, inc=1, device_id=peer(t)[1], device_id_type=MESH)

    def greet_line(t):
        other = (z + 1 + t // pcols) % planes
        pl.semaphore_signal(
            barrier, inc=1, device_id=(other * group + x, t % pcols), device_id_type=MESH
        )

    each((planes - 1) * pcols, greet_line)
    each(members, greet_plane, 1)

    for load in loads:
        load.wait()

    keep_lower = lax.broadcasted_iota(jnp.int32, (w, w), 0) >= lax.broadcasted_iota(
        jnp.int32, (w, w), 1
    )
    lower_one = jnp.where(keep_lower, inverse_one[0].astype(f32), 0.0).astype(bf16)
    lower_two = jnp.where(keep_lower, inverse_two[0].astype(f32), 0.0).astype(bf16)
    for k in range(tiles):
        msg[k] = dot(factor_one[0, k], lower_one).astype(bf16)
        msg[tiles + k] = dot(factor_two[0, k], lower_two).astype(bf16)
    part = parent_block[0, pl.ds(pl.multiple_of(c * slice_rows, slice_rows), slice_rows), :]
    par_msg[...] = dot(part, lower_two).astype(bf16)

    pl.semaphore_wait(barrier, (planes - 1) * pcols + members - 1)

    def msg_copy(t):
        other = (z + t) % planes
        return pltpu.make_async_remote_copy(
            src_ref=msg, dst_ref=rx.at[c], send_sem=msg_s.at[t], recv_sem=msg_r.at[c],
            device_id=(other * group + x, target_col), device_id_type=MESH,
        )

    def par_copy(t):
        other = (z + t) % planes
        return pltpu.make_async_remote_copy(
            src_ref=par_msg, dst_ref=par_rx.at[c], send_sem=par_s.at[t], recv_sem=par_r.at[c],
            device_id=(other * group + x, target_col), device_id_type=MESH,
        )

    stays = target_col == c
    for copy_to in (msg_copy, par_copy):
        each(planes, lambda t: copy_to(planes - t).start(), 1)

    @pl.when(jnp.logical_not(stays))
    def _():
        msg_copy(0).start()
        par_copy(0).start()

    @pl.when(stays)
    def _():
        pltpu.make_async_copy(msg, rx.at[c], msg_r.at[c]).start()
        pltpu.make_async_copy(par_msg, par_rx.at[c], par_r.at[c]).start()

    def sig_copy(t):
        return pltpu.make_async_remote_copy(
            src_ref=sigma.at[0], dst_ref=sig.at[x, own_cols], send_sem=sig_s.at[t],
            recv_sem=sig_r.at[m], device_id=peer(t)[1], device_id_type=MESH,
        )

    each(members, lambda t: sig_copy(t).start(), 1)

    def gram(lower):
        return jnp.where(mine, dot_t(lower, lower), 0.0)

    gram_one = gram(lower_one)
    gram_two = gram(lower_two)

    each(pcols, lambda t: pltpu.make_async_copy(rx.at[t], rx.at[t], msg_r.at[t]).wait())
    each(pcols, lambda t: pltpu.make_async_copy(par_rx.at[t], par_rx.at[t], par_r.at[t]).wait())

    up = parent[j]
    rows_one = [pattern[j, k] for k in range(reach)]
    rows_two = [pattern[up, k] for k in range(reach)]
    kept = [keep[j, k] for k in range(reach)]

    def find(rows, weights, b):
        column = tile = hit = jnp.int32(0)
        for k in range(reach):
            same = rows[k] == b
            if weights is not None:
                same = jnp.logical_and(same, weights[k] == 1)
            column = jnp.where(same, k // tiles, column)
            tile = jnp.where(same, k % tiles, tile)
            hit = jnp.where(same, 1, hit)
        return column, tile, hit.astype(f32)

    def fill(b):
        rows = pl.ds(pl.multiple_of(b * w, w), w)
        column, tile, hit = find(rows_one, None, b)
        spread[rows, 0:w] = (rx[column, tile].astype(f32) * hit).astype(bf16)
        column, tile, hit = find(rows_two, kept, b)
        spread[rows, w:2 * w] = (rx[column, tiles + tile].astype(f32) * hit).astype(bf16)

    each(tops, fill)
    scaled_parent = jnp.concatenate(
        [par_rx[t] for t in range(pcols)], axis=0
    )

    def sig_wait(t):
        q, _ = peer(t)
        ref = sig.at[q // pcols, pl.ds((q % pcols) * cols, cols)]
        pltpu.make_async_copy(ref, ref, sig_r.at[q]).wait()

    each(members, sig_wait, 1)

    chunk = 8 if tops % 8 == 0 else 1

    def product(b0):
        return [
            dot(
                jnp.concatenate([sig[g, b0 + b] for b in range(chunk)], axis=1),
                spread[pl.ds(pl.multiple_of(b0 * w, w), chunk * w), :],
            )
            for g in range(group)
        ]

    if tops == chunk:
        sums = product(0)
    else:
        total[...] = jnp.zeros_like(total)

        def add(n):
            for g, value in enumerate(product(n * chunk)):
                total[g] += value

        lax.fori_loop(0, tops // chunk, lambda n, carry: (add(n), carry)[1], 0)
        sums = [total[g] for g in range(group)]

    hits_one = [find(rows_one, None, z * group + g)[2] for g in range(group)]
    hits_two = [find(rows_two, kept, z * group + g)[2] for g in range(group)]
    own_rows = spread[pl.ds(pl.multiple_of(z * group * w, w), group * w), :]
    own_one, own_two = own_rows[:, 0:w], own_rows[:, w:2 * w]
    summed_one = jnp.concatenate([s[:, 0:w] for s in sums], axis=0)
    for g in range(group):
        ag[m, g] = (sums[g][:, 0:w] * -hits_one[g]).astype(bf16)
    part_one = (gram_one + dot_t(own_one, summed_one.astype(bf16))).astype(bf16)
    ag[m, group] = part_one
    z_one[...] = part_one

    def ag_copy(t):
        return pltpu.make_async_remote_copy(
            src_ref=ag.at[m], dst_ref=ag.at[m], send_sem=ag_s.at[t], recv_sem=ag_r.at[m],
            device_id=peer(t)[1], device_id_type=MESH,
        )

    each(members, lambda t: ag_copy(t).start(), 1)

    def z_copy(source, target, sem, recv):
        return pltpu.make_async_remote_copy(
            src_ref=source, dst_ref=target.at[z], send_sem=z_s.at[sem], recv_sem=recv.at[z],
            device_id=(home * group + x, c), device_id_type=MESH,
        )

    first = z_copy(z_one, zr_one, 0, zr_one_r)
    second = z_copy(z_two, zr_two, 1, zr_two_r)

    @pl.when(jnp.logical_not(mine))
    def _():
        first.start()

    def ag_wait(t):
        q, _ = peer(t)
        pltpu.make_async_copy(ag.at[q], ag.at[q], ag_r.at[q]).wait()

    each(members, ag_wait, 1)

    def out_one(row):
        return pltpu.make_async_copy(ag.at[place(row), x], top_one.at[0, row], store_s.at[row])

    each(tops, lambda row: out_one(row).start())

    slot = jnp.int32(0)
    for row in range(tops):
        slot = jnp.where(up == row, place(row), slot)
    inherited = jnp.concatenate([ag[slot, g] for g in range(group)], axis=0)
    up_diag = ag[slot, group]
    summed_two = jnp.concatenate([s[:, w:2 * w] for s in sums], axis=0) + dot(
        inherited, scaled_parent
    )
    carried = dot_t(inherited, own_two) + dot(up_diag, scaled_parent)
    part_two = (
        gram_two
        + dot_t(own_two, summed_two.astype(bf16))
        + dot_t(scaled_parent, carried.astype(bf16))
    )
    z_two[0] = carried.astype(bf16)
    z_two[1] = part_two.astype(bf16)

    @pl.when(jnp.logical_not(mine))
    def _():
        second.start()

    for g in range(group):
        two_send[g] = (summed_two[g * w:(g + 1) * w] * -hits_two[g]).astype(bf16)
    two_recv[m] = two_send[x]

    def two_copy(t):
        q, device = peer(t)
        return pltpu.make_async_remote_copy(
            src_ref=two_send.at[q // pcols], dst_ref=two_recv.at[m], send_sem=two_s.at[t],
            recv_sem=two_r.at[m], device_id=device, device_id_type=MESH,
        )

    each(members, lambda t: two_copy(t).start(), 1)

    def fin_copy(t):
        return pltpu.make_async_remote_copy(
            src_ref=fin, dst_ref=fin, send_sem=fin_s.at[t], recv_sem=fin_r,
            device_id=(p, (c + t) % pcols), device_id_type=MESH,
        )

    @pl.when(mine)
    def _():
        def gather_wait(ref, sem):
            def step(t):
                other = (z + t) % planes
                pltpu.make_async_copy(ref.at[other], ref.at[other], sem.at[other]).wait()
            each(planes, step, 1)

        gather_wait(zr_one, zr_one_r)
        zr_one[z] = z_one[...]
        fin[0] = jnp.sum(zr_one[...].astype(f32), axis=0).astype(bf16)
        gather_wait(zr_two, zr_two_r)
        zr_two[z] = z_two[...]
        fin[1:3] = jnp.sum(zr_two[...].astype(f32), axis=0).astype(bf16)
        each(pcols, lambda t: fin_copy(t).start(), 1)


    def two_wait(t):
        q, _ = peer(t)
        pltpu.make_async_copy(two_recv.at[q], two_recv.at[q], two_r.at[q]).wait()

    each(members, two_wait, 1)

    def out_two(row):
        return pltpu.make_async_copy(
            two_recv.at[place(row)], top_two.at[0, row], store_s.at[tops + row]
        )

    each(tops, lambda row: out_two(row).start())

    @pl.when(jnp.logical_not(mine))
    def _():
        pltpu.make_async_copy(fin, fin, fin_r).wait()

    blocks[0] = fin[0].astype(f32)
    blocks[1] = -fin[1].astype(f32)
    blocks[2] = fin[2].astype(f32)
    block_copies = [
        pltpu.make_async_copy(blocks.at[n], ref.at[0], store_s.at[2 * tops + n])
        for n, ref in enumerate((diag_one, parent_out, diag_two))
    ]
    for copy in block_copies:
        copy.start()

    each(tops, lambda row: out_one(row).wait())
    each(tops, lambda row: out_two(row).wait())
    for copy in block_copies:
        copy.wait()
    for copy_to in (msg_copy, par_copy):
        each(planes, lambda t: copy_to(planes - t).wait_send(), 1)

    @pl.when(jnp.logical_not(stays))
    def _():
        msg_copy(0).wait_send()
        par_copy(0).wait_send()

    def drain(t):
        sig_copy(t).wait_send()
        ag_copy(t).wait_send()
        two_copy(t).wait_send()

    each(members, drain, 1)

    @pl.when(jnp.logical_not(mine))
    def _():
        first.wait_send()
        second.wait_send()

    @pl.when(mine)
    def _():
        each(pcols, lambda t: fin_copy(t).wait_send(), 1)


def write_out(*refs):
    sources, targets, held = refs[0:5], refs[5:10], refs[10:15]
    loads = [pltpu.make_async_copy(sources[n], held[n], refs[15].at[n]) for n in range(5)]
    stores = [pltpu.make_async_copy(held[n], targets[n], refs[16].at[n]) for n in range(5)]
    for load in loads:
        load.start()
    for load, store in zip(loads, stores):
        load.wait()
        store.start()
    for store in stores:
        store.wait()


def body(
    prows, pcols,
    sigma_top, factor_one, inverse_one, pattern_one, factor_two, parent_block, inverse_two,
    parent_two, keep_two,
):
    w = sigma_top.shape[2]
    total_one = pattern_one.shape[0]
    tops = prows * sigma_top.shape[0]
    group = total_one // pcols
    planes = prows // group
    members = group * pcols
    tiles = factor_one.shape[1]
    assert sigma_top.shape[0] == factor_one.shape[0] == factor_two.shape[0] == 1
    assert planes == pcols and members == tops == total_one == parent_two.shape[0]
    hbm = pl.BlockSpec(memory_space=pltpu.HBM)
    shapes = (
        jax.ShapeDtypeStruct((1, total_one, w, w), bf16),
        jax.ShapeDtypeStruct((1, w, w), f32),
        jax.ShapeDtypeStruct((1, total_one, w, w), bf16),
        jax.ShapeDtypeStruct((1, w, w), f32),
        jax.ShapeDtypeStruct((1, w, w), f32),
    )
    dma = pltpu.SemaphoreType.DMA
    results = pl.pallas_call(
        functools.partial(kernel, prows, pcols, group),
        out_shape=shapes,
        in_specs=[hbm] * 9,
        out_specs=(hbm,) * 5,
        scratch_shapes=[
            pltpu.VMEM(factor_one.shape, bf16),
            pltpu.VMEM(inverse_one.shape, bf16),
            pltpu.VMEM(factor_two.shape, bf16),
            pltpu.VMEM(parent_block.shape, bf16),
            pltpu.VMEM(inverse_two.shape, bf16),
            pltpu.SMEM(pattern_one.shape, jnp.int32),
            pltpu.SMEM(parent_two.shape, jnp.int32),
            pltpu.SMEM(keep_two.shape, jnp.int32),
            dma((9,)),
            dma((2 * total_one + 3,)),
            pltpu.VMEM((3, w, w), f32),
            pltpu.VMEM((2 * tiles, w, w), bf16),
            pltpu.VMEM((w // pcols, w), bf16),
            pltpu.VMEM((pcols, 2 * tiles, w, w), bf16),
            pltpu.VMEM((pcols, w // pcols, w), bf16),
            pltpu.VMEM((group, tops, w, w), bf16),
            pltpu.VMEM((tops * w, 2 * w), bf16),
            pltpu.VMEM((group, w, 2 * w), f32),
            pltpu.VMEM((members, group + 1, w, w), bf16),
            pltpu.VMEM((group, w, w), bf16),
            pltpu.VMEM((members, w, w), bf16),
            pltpu.VMEM((w, w), bf16),
            pltpu.VMEM((2, w, w), bf16),
            pltpu.VMEM((planes, w, w), bf16),
            pltpu.VMEM((planes, 2, w, w), bf16),
            pltpu.VMEM((3, w, w), bf16),
            dma((planes,)), dma((planes,)), dma((pcols,)), dma((pcols,)),
            dma((members,)), dma((members,)),
            dma((members,)), dma((members,)),
            dma((members,)), dma((members,)),
            dma((2,)), dma((planes,)), dma((planes,)),
            dma((pcols,)), dma,
        ],
        compiler_params=pltpu.CompilerParams(
            collective_id=0, has_side_effects=True
        ),
    )(
        sigma_top, factor_one, inverse_one, factor_two, parent_block, inverse_two,
        pattern_one, parent_two, keep_two,
    )
    return pl.pallas_call(
        write_out,
        out_shape=shapes,
        in_specs=[hbm] * 5,
        out_specs=(hbm,) * 5,
        scratch_shapes=[pltpu.VMEM(s.shape, s.dtype) for s in shapes] + [dma((5,)), dma((5,))],
    )(*results)


def solution(mesh):
    in_specs = (
        P("prow", "pcol", None, None),
        P("prow", "pcol", None, None),
        P("prow", None, None),
        P(),
        P("prow", "pcol", None, None),
        P("prow", None, None),
        P("prow", None, None),
        P(),
        P(),
    )
    out_specs = (
        P("prow", None, None, None),
        P("prow", None, None),
        P("prow", None, None, None),
        P("prow", None, None),
        P("prow", None, None),
    )
    step = functools.partial(body, mesh.shape["prow"], mesh.shape["pcol"])
    return jax.shard_map(step, mesh=mesh, in_specs=in_specs, out_specs=out_specs, check_vma=False)
```

```python
import functools

import jax
import jax.numpy as jnp
from jax import lax
from jax.experimental import pallas as pl
from jax.experimental.pallas import tpu as pltpu
from jax.sharding import PartitionSpec as P

MESH = pl.DeviceIdType.MESH
f32 = jnp.float32
bf16 = jnp.bfloat16


def each(count, step, start=0):
    if count - start <= 8:
        for i in range(start, count):
            step(i)
    else:
        lax.fori_loop(start, count, lambda i, carry: (step(i), carry)[1], 0)


def dot(left, right):
    return jnp.dot(left, right, preferred_element_type=f32)


def dot_t(left, right):
    return dot(left.astype(f32).T.astype(bf16), right)


def kernel(
    prows, pcols, group,
    sigma, factor_one_in, inverse_one_in, factor_two_in, parent_block_in, inverse_two_in,
    pattern_in, parent_in, keep_in,
    top_one, diag_one, top_two, parent_out, diag_two,
    factor_one, inverse_one, factor_two, parent_block, inverse_two, pattern, parent, keep,
    load_s, store_s, blocks, msg, par_msg, rx, rx_two, par_rx, sig, spread_one, spread_two, total, ag, two_send, two_recv, z_one, z_two, zr_one, zr_two, fin,
    msg_s, msg_two_s, par_s, msg_r, msg_two_r, par_r, sig_s, sig_r, ag_s, ag_r, two_s, two_r, z_s, zr_one_r, zr_two_r, fin_s, fin_r,
):
    planes = prows // group
    half = pcols // 2
    cols = sigma.shape[1]
    w = sigma.shape[2]
    tiles = factor_one_in.shape[1]
    reach = pattern.shape[1]
    tops = prows
    members = group * pcols
    slice_rows = w // pcols

    p = lax.axis_index("prow")
    c = lax.axis_index("pcol")
    z, x = p // group, p % group
    m = x * pcols + c
    home = c // 2 + (c % 2) * half
    j = home * group + x
    mine = p == j
    target_col = (z % half) * 2 + z // half

    def place(row):
        plane = row // group
        return (row % group) * pcols + (plane % half) * 2 + plane // half

    def peer(t):
        q = (m + t) % members
        return q, (z * group + q // pcols, q % pcols)

    own_cols = pl.ds(c * cols, cols)
    loads = [
        pltpu.make_async_copy(source, target, load_s.at[n])
        for n, (source, target) in enumerate([
            (inverse_two_in, inverse_two), (factor_two_in, factor_two),
            (inverse_one_in, inverse_one), (factor_one_in, factor_one),
            (parent_block_in, parent_block), (sigma.at[0], sig.at[x, own_cols]),
            (pattern_in, pattern), (parent_in, parent), (keep_in, keep),
        ])
    ]
    for load in loads:
        load.start()

    chips = members // 2
    other_core = (z * group + x, c + 1 - 2 * (c % 2))

    def far(t):
        q = (m + 2 * t) % members
        return q, (z * group + q // pcols, q % pcols)

    def near(t):
        return (2 * (m // 2) + 1 - m % 2 + 2 * t) % members

    def plane_start(copy):
        each(chips, lambda t: copy(t, far(t)[1]).start(), 1)
        copy(0, other_core).start()

    def plane_wait(wait, forward):
        def pass_on(t):
            q, _ = far(t)
            wait(q)
            forward(t, q).start()

        each(chips, pass_on, 1)
        each(chips, lambda t: wait(near(t)))

    def plane_drain(copy, forward):
        def drain(t):
            copy(t, far(t)[1]).wait_send()
            forward(t, far(t)[0]).wait_send()

        each(chips, drain, 1)
        copy(0, other_core).wait_send()

    barrier = pltpu.get_barrier_semaphore()

    def greet_plane(t):
        pl.semaphore_signal(barrier, inc=1, device_id=peer(t)[1], device_id_type=MESH)

    def greet_line(t):
        other = (z + 1 + t // pcols) % planes
        pl.semaphore_signal(
            barrier, inc=1, device_id=(other * group + x, t % pcols), device_id_type=MESH
        )

    each((planes - 1) * pcols, greet_line)
    each(members, greet_plane, 1)

    for load in loads:
        load.wait()

    keep_lower = lax.broadcasted_iota(jnp.int32, (w, w), 0) >= lax.broadcasted_iota(
        jnp.int32, (w, w), 1
    )
    lower_one = jnp.where(keep_lower, inverse_one[0].astype(f32), 0.0).astype(bf16)
    lower_two = jnp.where(keep_lower, inverse_two[0].astype(f32), 0.0).astype(bf16)
    for k in range(tiles):
        msg[k] = dot(factor_one[0, k], lower_one).astype(bf16)
        msg[tiles + k] = dot(factor_two[0, k], lower_two).astype(bf16)
    part = parent_block[0, pl.ds(pl.multiple_of(c * slice_rows, slice_rows), slice_rows), :]
    par_msg[...] = dot(part, lower_two).astype(bf16)

    pl.semaphore_wait(barrier, (planes - 1) * pcols + members - 1)

    def msg_copy(t):
        other = (z + t) % planes
        return pltpu.make_async_remote_copy(
            src_ref=msg.at[0:tiles], dst_ref=rx.at[c], send_sem=msg_s.at[t],
            recv_sem=msg_r.at[c],
            device_id=(other * group + x, target_col), device_id_type=MESH,
        )

    def msg_two_copy(t):
        other = (z + t) % planes
        return pltpu.make_async_remote_copy(
            src_ref=msg.at[tiles:2 * tiles], dst_ref=rx_two.at[c],
            send_sem=msg_two_s.at[t], recv_sem=msg_two_r.at[c],
            device_id=(other * group + x, target_col), device_id_type=MESH,
        )

    def par_copy(t):
        other = (z + t) % planes
        return pltpu.make_async_remote_copy(
            src_ref=par_msg, dst_ref=par_rx.at[c], send_sem=par_s.at[t], recv_sem=par_r.at[c],
            device_id=(other * group + x, target_col), device_id_type=MESH,
        )

    stays = target_col == c

    def send_tiles(copies, local):
        for copy_to in copies:
            each(planes, lambda t: copy_to(planes - t).start(), 1)

        @pl.when(jnp.logical_not(stays))
        def _():
            for copy_to in copies:
                copy_to(0).start()

        @pl.when(stays)
        def _():
            for source, target, sem in local:
                pltpu.make_async_copy(source, target, sem).start()

    send_tiles([msg_copy], [(msg.at[0:tiles], rx.at[c], msg_r.at[c])])

    def sig_slot(q):
        return sig.at[q // pcols, pl.ds((q % pcols) * cols, cols)]

    def sig_copy(t, device):
        return pltpu.make_async_remote_copy(
            src_ref=sigma.at[0], dst_ref=sig_slot(m), send_sem=sig_s.at[t],
            recv_sem=sig_r.at[m], device_id=device, device_id_type=MESH,
        )

    def sig_forward(t, q):
        return pltpu.make_async_remote_copy(
            src_ref=sig_slot(q), dst_ref=sig_slot(q), send_sem=sig_s.at[chips + t],
            recv_sem=sig_r.at[q], device_id=other_core, device_id_type=MESH,
        )

    plane_start(sig_copy)

    def gram(lower):
        return jnp.where(mine, dot_t(lower, lower), 0.0)

    gram_one = gram(lower_one)
    gram_two = gram(lower_two)

    def tiles_wait(ref, sem):
        pltpu.make_async_copy(ref, ref, sem).wait()

    each(pcols, lambda t: tiles_wait(rx.at[t], msg_r.at[t]))
    send_tiles(
        [msg_two_copy, par_copy],
        [
            (msg.at[tiles:2 * tiles], rx_two.at[c], msg_two_r.at[c]),
            (par_msg, par_rx.at[c], par_r.at[c]),
        ],
    )

    up = parent[j]
    rows_one = [pattern[j, k] for k in range(reach)]
    rows_two = [pattern[up, k] for k in range(reach)]
    kept = [keep[j, k] for k in range(reach)]

    def find(rows, weights, b):
        column = tile = hit = jnp.int32(0)
        for k in range(reach):
            same = rows[k] == b
            if weights is not None:
                same = jnp.logical_and(same, weights[k] == 1)
            column = jnp.where(same, k // tiles, column)
            tile = jnp.where(same, k % tiles, tile)
            hit = jnp.where(same, 1, hit)
        return column, tile, hit.astype(f32)

    def fill(b):
        rows = pl.ds(pl.multiple_of(b * w, w), w)
        column, tile, hit = find(rows_one, None, b)
        spread_one[rows, :] = (rx[column, tile].astype(f32) * hit).astype(bf16)

    def fill_two(b):
        rows = pl.ds(pl.multiple_of(b * w, w), w)
        column, tile, hit = find(rows_two, kept, b)
        spread_two[rows, :] = (rx_two[column, tile].astype(f32) * hit).astype(bf16)

    each(tops, fill)
    def sig_wait(q):
        pltpu.make_async_copy(sig_slot(q), sig_slot(q), sig_r.at[q]).wait()

    plane_wait(sig_wait, sig_forward)

    chunk = 8 if tops % 8 == 0 else 1

    def product(spread, b0):
        return [
            dot(
                jnp.concatenate([sig[g, b0 + b] for b in range(chunk)], axis=1),
                spread[pl.ds(pl.multiple_of(b0 * w, w), chunk * w), :],
            )
            for g in range(group)
        ]

    def products(spread):
        if tops == chunk:
            return jnp.concatenate(product(spread, 0), axis=0)
        total[...] = jnp.zeros_like(total)

        def add(n):
            for g, value in enumerate(product(spread, n * chunk)):
                total[g] += value

        lax.fori_loop(0, tops // chunk, lambda n, carry: (add(n), carry)[1], 0)
        return jnp.concatenate([total[g] for g in range(group)], axis=0)

    summed_one = products(spread_one)
    hits_one = [find(rows_one, None, z * group + g)[2] for g in range(group)]
    hits_two = [find(rows_two, kept, z * group + g)[2] for g in range(group)]
    own = pl.ds(pl.multiple_of(z * group * w, w), group * w)
    own_one = spread_one[own, :]
    for g in range(group):
        ag[m, g] = (summed_one[g * w:(g + 1) * w] * -hits_one[g]).astype(bf16)
    part_one = (gram_one + dot_t(own_one, summed_one.astype(bf16))).astype(bf16)
    ag[m, group] = part_one
    z_one[...] = part_one

    def ag_copy(t, device):
        return pltpu.make_async_remote_copy(
            src_ref=ag.at[m], dst_ref=ag.at[m], send_sem=ag_s.at[t], recv_sem=ag_r.at[m],
            device_id=device, device_id_type=MESH,
        )

    def ag_forward(t, q):
        return pltpu.make_async_remote_copy(
            src_ref=ag.at[q], dst_ref=ag.at[q], send_sem=ag_s.at[chips + t],
            recv_sem=ag_r.at[q], device_id=other_core, device_id_type=MESH,
        )

    plane_start(ag_copy)

    def z_copy(source, target, sem, recv):
        return pltpu.make_async_remote_copy(
            src_ref=source, dst_ref=target.at[z], send_sem=z_s.at[sem], recv_sem=recv.at[z],
            device_id=(home * group + x, c), device_id_type=MESH,
        )

    first = z_copy(z_one, zr_one, 0, zr_one_r)
    second = z_copy(z_two, zr_two, 1, zr_two_r)

    @pl.when(jnp.logical_not(mine))
    def _():
        first.start()

    def ag_wait(q):
        pltpu.make_async_copy(ag.at[q], ag.at[q], ag_r.at[q]).wait()

    each(pcols, lambda t: tiles_wait(rx_two.at[t], msg_two_r.at[t]))
    each(pcols, lambda t: tiles_wait(par_rx.at[t], par_r.at[t]))
    each(tops, fill_two)
    own_two = spread_two[own, :]
    scaled_parent = jnp.concatenate(
        [par_rx[t] for t in range(pcols)], axis=0
    )

    base_two = products(spread_two)

    plane_wait(ag_wait, ag_forward)

    def out_one(row):
        return pltpu.make_async_copy(ag.at[place(row), x], top_one.at[0, row], store_s.at[row])

    each(tops, lambda row: out_one(row).start())

    slot = jnp.int32(0)
    for row in range(tops):
        slot = jnp.where(up == row, place(row), slot)
    inherited = jnp.concatenate([ag[slot, g] for g in range(group)], axis=0)
    up_diag = ag[slot, group]
    summed_two = base_two + dot(inherited, scaled_parent)
    carried = dot_t(inherited, own_two) + dot(up_diag, scaled_parent)
    part_two = (
        gram_two
        + dot_t(own_two, summed_two.astype(bf16))
        + dot_t(scaled_parent, carried.astype(bf16))
    )
    z_two[0] = carried.astype(bf16)
    z_two[1] = part_two.astype(bf16)

    @pl.when(jnp.logical_not(mine))
    def _():
        second.start()

    for g in range(group):
        two_send[g] = (summed_two[g * w:(g + 1) * w] * -hits_two[g]).astype(bf16)
    two_recv[m] = two_send[x]

    def two_copy(t):
        q, device = peer(t)
        return pltpu.make_async_remote_copy(
            src_ref=two_send.at[q // pcols], dst_ref=two_recv.at[m], send_sem=two_s.at[t],
            recv_sem=two_r.at[m], device_id=device, device_id_type=MESH,
        )

    each(members, lambda t: two_copy(t).start(), 1)

    def fin_copy(t):
        return pltpu.make_async_remote_copy(
            src_ref=fin, dst_ref=fin, send_sem=fin_s.at[t], recv_sem=fin_r,
            device_id=(p, (c + t) % pcols), device_id_type=MESH,
        )

    @pl.when(mine)
    def _():
        def gather_wait(ref, sem):
            def step(t):
                other = (z + t) % planes
                pltpu.make_async_copy(ref.at[other], ref.at[other], sem.at[other]).wait()
            each(planes, step, 1)

        gather_wait(zr_one, zr_one_r)
        zr_one[z] = z_one[...]
        fin[0] = jnp.sum(zr_one[...].astype(f32), axis=0).astype(bf16)
        gather_wait(zr_two, zr_two_r)
        zr_two[z] = z_two[...]
        fin[1:3] = jnp.sum(zr_two[...].astype(f32), axis=0).astype(bf16)
        each(pcols, lambda t: fin_copy(t).start(), 1)


    def two_wait(t):
        q, _ = peer(t)
        pltpu.make_async_copy(two_recv.at[q], two_recv.at[q], two_r.at[q]).wait()

    each(members, two_wait, 1)

    def out_two(row):
        return pltpu.make_async_copy(
            two_recv.at[place(row)], top_two.at[0, row], store_s.at[tops + row]
        )

    each(tops, lambda row: out_two(row).start())

    @pl.when(jnp.logical_not(mine))
    def _():
        pltpu.make_async_copy(fin, fin, fin_r).wait()

    blocks[0] = fin[0].astype(f32)
    blocks[1] = -fin[1].astype(f32)
    blocks[2] = fin[2].astype(f32)
    block_copies = [
        pltpu.make_async_copy(blocks.at[n], ref.at[0], store_s.at[2 * tops + n])
        for n, ref in enumerate((diag_one, parent_out, diag_two))
    ]
    for copy in block_copies:
        copy.start()

    each(tops, lambda row: out_one(row).wait())
    each(tops, lambda row: out_two(row).wait())
    for copy in block_copies:
        copy.wait()
    for copy_to in (msg_copy, msg_two_copy, par_copy):
        each(planes, lambda t: copy_to(planes - t).wait_send(), 1)

    @pl.when(jnp.logical_not(stays))
    def _():
        msg_copy(0).wait_send()
        msg_two_copy(0).wait_send()
        par_copy(0).wait_send()

    def drain(t):
        two_copy(t).wait_send()

    each(members, drain, 1)
    plane_drain(sig_copy, sig_forward)
    plane_drain(ag_copy, ag_forward)

    @pl.when(jnp.logical_not(mine))
    def _():
        first.wait_send()
        second.wait_send()

    @pl.when(mine)
    def _():
        each(pcols, lambda t: fin_copy(t).wait_send(), 1)


def write_out(*refs):
    sources, targets, held = refs[0:5], refs[5:10], refs[10:15]
    loads = [pltpu.make_async_copy(sources[n], held[n], refs[15].at[n]) for n in range(5)]
    stores = [pltpu.make_async_copy(held[n], targets[n], refs[16].at[n]) for n in range(5)]
    for load in loads:
        load.start()
    for load, store in zip(loads, stores):
        load.wait()
        store.start()
    for store in stores:
        store.wait()


def body(
    prows, pcols,
    sigma_top, factor_one, inverse_one, pattern_one, factor_two, parent_block, inverse_two,
    parent_two, keep_two,
):
    w = sigma_top.shape[2]
    total_one = pattern_one.shape[0]
    tops = prows * sigma_top.shape[0]
    group = total_one // pcols
    planes = prows // group
    members = group * pcols
    tiles = factor_one.shape[1]
    assert sigma_top.shape[0] == factor_one.shape[0] == factor_two.shape[0] == 1
    assert planes == pcols and members == tops == total_one == parent_two.shape[0]
    hbm = pl.BlockSpec(memory_space=pltpu.HBM)
    shapes = (
        jax.ShapeDtypeStruct((1, total_one, w, w), bf16),
        jax.ShapeDtypeStruct((1, w, w), f32),
        jax.ShapeDtypeStruct((1, total_one, w, w), bf16),
        jax.ShapeDtypeStruct((1, w, w), f32),
        jax.ShapeDtypeStruct((1, w, w), f32),
    )
    dma = pltpu.SemaphoreType.DMA
    results = pl.pallas_call(
        functools.partial(kernel, prows, pcols, group),
        out_shape=shapes,
        in_specs=[hbm] * 9,
        out_specs=(hbm,) * 5,
        scratch_shapes=[
            pltpu.VMEM(factor_one.shape, bf16),
            pltpu.VMEM(inverse_one.shape, bf16),
            pltpu.VMEM(factor_two.shape, bf16),
            pltpu.VMEM(parent_block.shape, bf16),
            pltpu.VMEM(inverse_two.shape, bf16),
            pltpu.SMEM(pattern_one.shape, jnp.int32),
            pltpu.SMEM(parent_two.shape, jnp.int32),
            pltpu.SMEM(keep_two.shape, jnp.int32),
            dma((9,)),
            dma((2 * total_one + 3,)),
            pltpu.VMEM((3, w, w), f32),
            pltpu.VMEM((2 * tiles, w, w), bf16),
            pltpu.VMEM((w // pcols, w), bf16),
            pltpu.VMEM((pcols, tiles, w, w), bf16),
            pltpu.VMEM((pcols, tiles, w, w), bf16),
            pltpu.VMEM((pcols, w // pcols, w), bf16),
            pltpu.VMEM((group, tops, w, w), bf16),
            pltpu.VMEM((tops * w, w), bf16),
            pltpu.VMEM((tops * w, w), bf16),
            pltpu.VMEM((group, w, w), f32),
            pltpu.VMEM((members, group + 1, w, w), bf16),
            pltpu.VMEM((group, w, w), bf16),
            pltpu.VMEM((members, w, w), bf16),
            pltpu.VMEM((w, w), bf16),
            pltpu.VMEM((2, w, w), bf16),
            pltpu.VMEM((planes, w, w), bf16),
            pltpu.VMEM((planes, 2, w, w), bf16),
            pltpu.VMEM((3, w, w), bf16),
            dma((planes,)), dma((planes,)), dma((planes,)),
            dma((pcols,)), dma((pcols,)), dma((pcols,)),
            dma((members,)), dma((members,)),
            dma((members,)), dma((members,)),
            dma((members,)), dma((members,)),
            dma((2,)), dma((planes,)), dma((planes,)),
            dma((pcols,)), dma,
        ],
        compiler_params=pltpu.CompilerParams(
            collective_id=0, has_side_effects=True
        ),
    )(
        sigma_top, factor_one, inverse_one, factor_two, parent_block, inverse_two,
        pattern_one, parent_two, keep_two,
    )
    return pl.pallas_call(
        write_out,
        out_shape=shapes,
        in_specs=[hbm] * 5,
        out_specs=(hbm,) * 5,
        scratch_shapes=[pltpu.VMEM(s.shape, s.dtype) for s in shapes] + [dma((5,)), dma((5,))],
    )(*results)


def solution(mesh):
    in_specs = (
        P("prow", "pcol", None, None),
        P("prow", "pcol", None, None),
        P("prow", None, None),
        P(),
        P("prow", "pcol", None, None),
        P("prow", None, None),
        P("prow", None, None),
        P(),
        P(),
    )
    out_specs = (
        P("prow", None, None, None),
        P("prow", None, None),
        P("prow", None, None, None),
        P("prow", None, None),
        P("prow", None, None),
    )
    step = functools.partial(body, mesh.shape["prow"], mesh.shape["pcol"])
    return jax.shard_map(step, mesh=mesh, in_specs=in_specs, out_specs=out_specs, check_vma=False)
```

```python
import functools

import jax
import jax.numpy as jnp
from jax import lax
from jax.experimental import pallas as pl
from jax.experimental.pallas import tpu as pltpu
from jax.sharding import PartitionSpec as P

MESH = pl.DeviceIdType.MESH
f32 = jnp.float32
bf16 = jnp.bfloat16


def each(count, step, start=0):
    if count - start <= 8:
        for i in range(start, count):
            step(i)
    else:
        lax.fori_loop(start, count, lambda i, carry: (step(i), carry)[1], 0)


def dot(left, right):
    return jnp.dot(left, right, preferred_element_type=f32)


def dot_t(left, right):
    return dot(left.astype(f32).T.astype(bf16), right)


def kernel(
    prows, pcols, group,
    sigma, factor_one_in, inverse_one_in, factor_two_in, parent_block_in, inverse_two_in,
    pattern_in, parent_in, keep_in,
    top_one, diag_one, top_two, parent_out, diag_two,
    factor_one, inverse_one, factor_two, parent_block, inverse_two, pattern, parent, keep,
    load_s, store_s, blocks, msg, par_msg, rx, rx_two, par_rx, sig, spread_one, spread_two, total, ag, two_send, two_recv, z_one, z_two, zr_one, zr_two, fin,
    msg_s, msg_two_s, par_s, msg_r, msg_two_r, par_r, sig_s, sig_r, ag_s, ag_r, two_s, two_r, z_s, zr_one_r, zr_two_r, fin_s, fin_r,
):
    planes = prows // group
    half = pcols // 2
    cols = sigma.shape[1]
    w = sigma.shape[2]
    tiles = factor_one_in.shape[1]
    reach = pattern.shape[1]
    tops = prows
    members = group * pcols
    slice_rows = w // pcols

    p = lax.axis_index("prow")
    c = lax.axis_index("pcol")
    z, x = p // group, p % group
    m = x * pcols + c
    home = c // 2 + (c % 2) * half
    j = home * group + x
    mine = p == j
    target_col = (z % half) * 2 + z // half

    def place(row):
        plane = row // group
        return (row % group) * pcols + (plane % half) * 2 + plane // half

    def peer(t):
        q = (m + t) % members
        return q, (z * group + q // pcols, q % pcols)

    own_cols = pl.ds(c * cols, cols)
    loads = [
        pltpu.make_async_copy(source, target, load_s.at[n])
        for n, (source, target) in enumerate([
            (inverse_two_in, inverse_two), (factor_two_in, factor_two),
            (inverse_one_in, inverse_one), (factor_one_in, factor_one),
            (parent_block_in, parent_block), (sigma.at[0], sig.at[x, own_cols]),
            (pattern_in, pattern), (parent_in, parent), (keep_in, keep),
        ])
    ]
    for load in loads:
        load.start()

    chips = members // 2
    other_core = (z * group + x, c + 1 - 2 * (c % 2))

    def far(t):
        q = (m + 2 * t) % members
        return q, (z * group + q // pcols, q % pcols)

    def near(t):
        return (2 * (m // 2) + 1 - m % 2 + 2 * t) % members

    def plane_start(copy):
        each(chips, lambda t: copy(t, far(t)[1]).start(), 1)
        copy(0, other_core).start()

    def plane_pass(wait, forward):
        def pass_on(t):
            q, _ = far(t)
            wait(q)
            forward(t, q).start()

        each(chips, pass_on, 1)

    def plane_rest(wait):
        each(chips, lambda t: wait(near(t)))

    def plane_drain(copy, forward):
        def drain(t):
            copy(t, far(t)[1]).wait_send()
            forward(t, far(t)[0]).wait_send()

        each(chips, drain, 1)
        copy(0, other_core).wait_send()

    barrier = pltpu.get_barrier_semaphore()

    def greet_plane(t):
        pl.semaphore_signal(barrier, inc=1, device_id=peer(t)[1], device_id_type=MESH)

    def greet_line(t):
        other = (z + 1 + t // pcols) % planes
        pl.semaphore_signal(
            barrier, inc=1, device_id=(other * group + x, t % pcols), device_id_type=MESH
        )

    each((planes - 1) * pcols, greet_line)
    each(members, greet_plane, 1)

    for load in loads:
        load.wait()

    keep_lower = lax.broadcasted_iota(jnp.int32, (w, w), 0) >= lax.broadcasted_iota(
        jnp.int32, (w, w), 1
    )
    lower_one = jnp.where(keep_lower, inverse_one[0].astype(f32), 0.0).astype(bf16)
    lower_two = jnp.where(keep_lower, inverse_two[0].astype(f32), 0.0).astype(bf16)
    for k in range(tiles):
        msg[k] = dot(factor_one[0, k], lower_one).astype(bf16)
        msg[tiles + k] = dot(factor_two[0, k], lower_two).astype(bf16)
    part = parent_block[0, pl.ds(pl.multiple_of(c * slice_rows, slice_rows), slice_rows), :]
    par_msg[...] = dot(part, lower_two).astype(bf16)

    pl.semaphore_wait(barrier, (planes - 1) * pcols + members - 1)

    def msg_copy(t):
        other = (z + t) % planes
        return pltpu.make_async_remote_copy(
            src_ref=msg.at[0:tiles], dst_ref=rx.at[c], send_sem=msg_s.at[t],
            recv_sem=msg_r.at[c],
            device_id=(other * group + x, target_col), device_id_type=MESH,
        )

    def msg_two_copy(t):
        other = (z + t) % planes
        return pltpu.make_async_remote_copy(
            src_ref=msg.at[tiles:2 * tiles], dst_ref=rx_two.at[c],
            send_sem=msg_two_s.at[t], recv_sem=msg_two_r.at[c],
            device_id=(other * group + x, target_col), device_id_type=MESH,
        )

    def par_copy(t):
        other = (z + t) % planes
        return pltpu.make_async_remote_copy(
            src_ref=par_msg, dst_ref=par_rx.at[c], send_sem=par_s.at[t], recv_sem=par_r.at[c],
            device_id=(other * group + x, target_col), device_id_type=MESH,
        )

    stays = target_col == c

    def send_tiles(copies, local):
        for copy_to in copies:
            each(planes, lambda t: copy_to(planes - t).start(), 1)

        @pl.when(jnp.logical_not(stays))
        def _():
            for copy_to in copies:
                copy_to(0).start()

        @pl.when(stays)
        def _():
            for source, target, sem in local:
                pltpu.make_async_copy(source, target, sem).start()

    send_tiles([msg_copy], [(msg.at[0:tiles], rx.at[c], msg_r.at[c])])

    def sig_slot(q):
        return sig.at[q // pcols, pl.ds((q % pcols) * cols, cols)]

    def sig_copy(t, device):
        return pltpu.make_async_remote_copy(
            src_ref=sigma.at[0], dst_ref=sig_slot(m), send_sem=sig_s.at[t],
            recv_sem=sig_r.at[m], device_id=device, device_id_type=MESH,
        )

    def sig_forward(t, q):
        return pltpu.make_async_remote_copy(
            src_ref=sig_slot(q), dst_ref=sig_slot(q), send_sem=sig_s.at[chips + t],
            recv_sem=sig_r.at[q], device_id=other_core, device_id_type=MESH,
        )

    def sig_wait(q):
        pltpu.make_async_copy(sig_slot(q), sig_slot(q), sig_r.at[q]).wait()

    plane_start(sig_copy)

    def gram(lower):
        return jnp.where(mine, dot_t(lower, lower), 0.0)

    gram_one = gram(lower_one)
    gram_two = gram(lower_two)

    def tiles_wait(ref, sem):
        pltpu.make_async_copy(ref, ref, sem).wait()

    plane_pass(sig_wait, sig_forward)
    each(pcols, lambda t: tiles_wait(rx.at[t], msg_r.at[t]))
    send_tiles(
        [msg_two_copy, par_copy],
        [
            (msg.at[tiles:2 * tiles], rx_two.at[c], msg_two_r.at[c]),
            (par_msg, par_rx.at[c], par_r.at[c]),
        ],
    )

    up = parent[j]
    rows_one = [pattern[j, k] for k in range(reach)]
    rows_two = [pattern[up, k] for k in range(reach)]
    kept = [keep[j, k] for k in range(reach)]

    def find(rows, weights, b):
        column = tile = hit = jnp.int32(0)
        for k in range(reach):
            same = rows[k] == b
            if weights is not None:
                same = jnp.logical_and(same, weights[k] == 1)
            column = jnp.where(same, k // tiles, column)
            tile = jnp.where(same, k % tiles, tile)
            hit = jnp.where(same, 1, hit)
        return column, tile, hit.astype(f32)

    def fill(b):
        rows = pl.ds(pl.multiple_of(b * w, w), w)
        column, tile, hit = find(rows_one, None, b)
        spread_one[rows, :] = (rx[column, tile].astype(f32) * hit).astype(bf16)

    def fill_two(b):
        rows = pl.ds(pl.multiple_of(b * w, w), w)
        column, tile, hit = find(rows_two, kept, b)
        spread_two[rows, :] = (rx_two[column, tile].astype(f32) * hit).astype(bf16)

    each(tops, fill)
    plane_rest(sig_wait)

    chunk = 8 if tops % 8 == 0 else 1

    def product(spread, b0):
        return [
            dot(
                jnp.concatenate([sig[g, b0 + b] for b in range(chunk)], axis=1),
                spread[pl.ds(pl.multiple_of(b0 * w, w), chunk * w), :],
            )
            for g in range(group)
        ]

    def products(spread):
        if tops == chunk:
            return jnp.concatenate(product(spread, 0), axis=0)
        total[...] = jnp.zeros_like(total)

        def add(n):
            for g, value in enumerate(product(spread, n * chunk)):
                total[g] += value

        lax.fori_loop(0, tops // chunk, lambda n, carry: (add(n), carry)[1], 0)
        return jnp.concatenate([total[g] for g in range(group)], axis=0)

    summed_one = products(spread_one)
    hits_one = [find(rows_one, None, z * group + g)[2] for g in range(group)]
    hits_two = [find(rows_two, kept, z * group + g)[2] for g in range(group)]
    own = pl.ds(pl.multiple_of(z * group * w, w), group * w)
    own_one = spread_one[own, :]
    for g in range(group):
        ag[m, g] = (summed_one[g * w:(g + 1) * w] * -hits_one[g]).astype(bf16)
    part_one = (gram_one + dot_t(own_one, summed_one.astype(bf16))).astype(bf16)
    ag[m, group] = part_one
    z_one[...] = part_one

    def ag_copy(t, device):
        return pltpu.make_async_remote_copy(
            src_ref=ag.at[m], dst_ref=ag.at[m], send_sem=ag_s.at[t], recv_sem=ag_r.at[m],
            device_id=device, device_id_type=MESH,
        )

    def ag_forward(t, q):
        return pltpu.make_async_remote_copy(
            src_ref=ag.at[q], dst_ref=ag.at[q], send_sem=ag_s.at[chips + t],
            recv_sem=ag_r.at[q], device_id=other_core, device_id_type=MESH,
        )

    plane_start(ag_copy)

    def z_copy(source, target, sem, recv):
        return pltpu.make_async_remote_copy(
            src_ref=source, dst_ref=target.at[z], send_sem=z_s.at[sem], recv_sem=recv.at[z],
            device_id=(home * group + x, c), device_id_type=MESH,
        )

    first = z_copy(z_one, zr_one, 0, zr_one_r)
    second = z_copy(z_two, zr_two, 1, zr_two_r)

    @pl.when(jnp.logical_not(mine))
    def _():
        first.start()

    def ag_wait(q):
        pltpu.make_async_copy(ag.at[q], ag.at[q], ag_r.at[q]).wait()

    plane_pass(ag_wait, ag_forward)

    each(pcols, lambda t: tiles_wait(rx_two.at[t], msg_two_r.at[t]))
    each(pcols, lambda t: tiles_wait(par_rx.at[t], par_r.at[t]))
    each(tops, fill_two)
    own_two = spread_two[own, :]
    scaled_parent = jnp.concatenate(
        [par_rx[t] for t in range(pcols)], axis=0
    )

    base_two = products(spread_two)

    plane_rest(ag_wait)

    def out_one(row):
        return pltpu.make_async_copy(ag.at[place(row), x], top_one.at[0, row], store_s.at[row])

    each(tops, lambda row: out_one(row).start())

    slot = jnp.int32(0)
    for row in range(tops):
        slot = jnp.where(up == row, place(row), slot)
    inherited = jnp.concatenate([ag[slot, g] for g in range(group)], axis=0)
    up_diag = ag[slot, group]
    summed_two = base_two + dot(inherited, scaled_parent)
    carried = dot_t(inherited, own_two) + dot(up_diag, scaled_parent)
    part_two = (
        gram_two
        + dot_t(own_two, summed_two.astype(bf16))
        + dot_t(scaled_parent, carried.astype(bf16))
    )
    z_two[0] = carried.astype(bf16)
    z_two[1] = part_two.astype(bf16)

    @pl.when(jnp.logical_not(mine))
    def _():
        second.start()

    for g in range(group):
        two_send[g] = (summed_two[g * w:(g + 1) * w] * -hits_two[g]).astype(bf16)
    two_recv[m] = two_send[x]

    def two_copy(t):
        q, device = peer(t)
        return pltpu.make_async_remote_copy(
            src_ref=two_send.at[q // pcols], dst_ref=two_recv.at[m], send_sem=two_s.at[t],
            recv_sem=two_r.at[m], device_id=device, device_id_type=MESH,
        )

    each(members, lambda t: two_copy(t).start(), 1)

    def fin_copy(t):
        return pltpu.make_async_remote_copy(
            src_ref=fin, dst_ref=fin, send_sem=fin_s.at[t], recv_sem=fin_r,
            device_id=(p, (c + t) % pcols), device_id_type=MESH,
        )

    @pl.when(mine)
    def _():
        def gather_wait(ref, sem):
            def step(t):
                other = (z + t) % planes
                pltpu.make_async_copy(ref.at[other], ref.at[other], sem.at[other]).wait()
            each(planes, step, 1)

        gather_wait(zr_one, zr_one_r)
        zr_one[z] = z_one[...]
        fin[0] = jnp.sum(zr_one[...].astype(f32), axis=0).astype(bf16)
        gather_wait(zr_two, zr_two_r)
        zr_two[z] = z_two[...]
        fin[1:3] = jnp.sum(zr_two[...].astype(f32), axis=0).astype(bf16)
        each(pcols, lambda t: fin_copy(t).start(), 1)


    def two_wait(t):
        q, _ = peer(t)
        pltpu.make_async_copy(two_recv.at[q], two_recv.at[q], two_r.at[q]).wait()

    each(members, two_wait, 1)

    def out_two(row):
        return pltpu.make_async_copy(
            two_recv.at[place(row)], top_two.at[0, row], store_s.at[tops + row]
        )

    each(tops, lambda row: out_two(row).start())

    @pl.when(jnp.logical_not(mine))
    def _():
        pltpu.make_async_copy(fin, fin, fin_r).wait()

    blocks[0] = fin[0].astype(f32)
    blocks[1] = -fin[1].astype(f32)
    blocks[2] = fin[2].astype(f32)
    block_copies = [
        pltpu.make_async_copy(blocks.at[n], ref.at[0], store_s.at[2 * tops + n])
        for n, ref in enumerate((diag_one, parent_out, diag_two))
    ]
    for copy in block_copies:
        copy.start()

    each(tops, lambda row: out_one(row).wait())
    each(tops, lambda row: out_two(row).wait())
    for copy in block_copies:
        copy.wait()
    for copy_to in (msg_copy, msg_two_copy, par_copy):
        each(planes, lambda t: copy_to(planes - t).wait_send(), 1)

    @pl.when(jnp.logical_not(stays))
    def _():
        msg_copy(0).wait_send()
        msg_two_copy(0).wait_send()
        par_copy(0).wait_send()

    def drain(t):
        two_copy(t).wait_send()

    each(members, drain, 1)
    plane_drain(sig_copy, sig_forward)
    plane_drain(ag_copy, ag_forward)

    @pl.when(jnp.logical_not(mine))
    def _():
        first.wait_send()
        second.wait_send()

    @pl.when(mine)
    def _():
        each(pcols, lambda t: fin_copy(t).wait_send(), 1)


def write_out(*refs):
    sources, targets, held = refs[0:5], refs[5:10], refs[10:15]
    loads = [pltpu.make_async_copy(sources[n], held[n], refs[15].at[n]) for n in range(5)]
    stores = [pltpu.make_async_copy(held[n], targets[n], refs[16].at[n]) for n in range(5)]
    for load in loads:
        load.start()
    for load, store in zip(loads, stores):
        load.wait()
        store.start()
    for store in stores:
        store.wait()


def body(
    prows, pcols,
    sigma_top, factor_one, inverse_one, pattern_one, factor_two, parent_block, inverse_two,
    parent_two, keep_two,
):
    w = sigma_top.shape[2]
    total_one = pattern_one.shape[0]
    tops = prows * sigma_top.shape[0]
    group = total_one // pcols
    planes = prows // group
    members = group * pcols
    tiles = factor_one.shape[1]
    assert sigma_top.shape[0] == factor_one.shape[0] == factor_two.shape[0] == 1
    assert planes == pcols and members == tops == total_one == parent_two.shape[0]
    hbm = pl.BlockSpec(memory_space=pltpu.HBM)
    shapes = (
        jax.ShapeDtypeStruct((1, total_one, w, w), bf16),
        jax.ShapeDtypeStruct((1, w, w), f32),
        jax.ShapeDtypeStruct((1, total_one, w, w), bf16),
        jax.ShapeDtypeStruct((1, w, w), f32),
        jax.ShapeDtypeStruct((1, w, w), f32),
    )
    dma = pltpu.SemaphoreType.DMA
    results = pl.pallas_call(
        functools.partial(kernel, prows, pcols, group),
        out_shape=shapes,
        in_specs=[hbm] * 9,
        out_specs=(hbm,) * 5,
        scratch_shapes=[
            pltpu.VMEM(factor_one.shape, bf16),
            pltpu.VMEM(inverse_one.shape, bf16),
            pltpu.VMEM(factor_two.shape, bf16),
            pltpu.VMEM(parent_block.shape, bf16),
            pltpu.VMEM(inverse_two.shape, bf16),
            pltpu.SMEM(pattern_one.shape, jnp.int32),
            pltpu.SMEM(parent_two.shape, jnp.int32),
            pltpu.SMEM(keep_two.shape, jnp.int32),
            dma((9,)),
            dma((2 * total_one + 3,)),
            pltpu.VMEM((3, w, w), f32),
            pltpu.VMEM((2 * tiles, w, w), bf16),
            pltpu.VMEM((w // pcols, w), bf16),
            pltpu.VMEM((pcols, tiles, w, w), bf16),
            pltpu.VMEM((pcols, tiles, w, w), bf16),
            pltpu.VMEM((pcols, w // pcols, w), bf16),
            pltpu.VMEM((group, tops, w, w), bf16),
            pltpu.VMEM((tops * w, w), bf16),
            pltpu.VMEM((tops * w, w), bf16),
            pltpu.VMEM((group, w, w), f32),
            pltpu.VMEM((members, group + 1, w, w), bf16),
            pltpu.VMEM((group, w, w), bf16),
            pltpu.VMEM((members, w, w), bf16),
            pltpu.VMEM((w, w), bf16),
            pltpu.VMEM((2, w, w), bf16),
            pltpu.VMEM((planes, w, w), bf16),
            pltpu.VMEM((planes, 2, w, w), bf16),
            pltpu.VMEM((3, w, w), bf16),
            dma((planes,)), dma((planes,)), dma((planes,)),
            dma((pcols,)), dma((pcols,)), dma((pcols,)),
            dma((members,)), dma((members,)),
            dma((members,)), dma((members,)),
            dma((members,)), dma((members,)),
            dma((2,)), dma((planes,)), dma((planes,)),
            dma((pcols,)), dma,
        ],
        compiler_params=pltpu.CompilerParams(
            collective_id=0, has_side_effects=True
        ),
    )(
        sigma_top, factor_one, inverse_one, factor_two, parent_block, inverse_two,
        pattern_one, parent_two, keep_two,
    )
    return pl.pallas_call(
        write_out,
        out_shape=shapes,
        in_specs=[hbm] * 5,
        out_specs=(hbm,) * 5,
        scratch_shapes=[pltpu.VMEM(s.shape, s.dtype) for s in shapes] + [dma((5,)), dma((5,))],
    )(*results)


def solution(mesh):
    in_specs = (
        P("prow", "pcol", None, None),
        P("prow", "pcol", None, None),
        P("prow", None, None),
        P(),
        P("prow", "pcol", None, None),
        P("prow", None, None),
        P("prow", None, None),
        P(),
        P(),
    )
    out_specs = (
        P("prow", None, None, None),
        P("prow", None, None),
        P("prow", None, None, None),
        P("prow", None, None),
        P("prow", None, None),
    )
    step = functools.partial(body, mesh.shape["prow"], mesh.shape["pcol"])
    return jax.shard_map(step, mesh=mesh, in_specs=in_specs, out_specs=out_specs, check_vma=False)
```
